32 devices in a mesh: lat: 4 (over x, core), lon: 8 (over z, y).
Axes of the slice: x: 2, y: 2, z: 4, core: 2. Of those that a mesh axis runs over, the one named last changes fastest.
Arguments:
- spectra: bfloat16 [98304, 616], P(('lat', 'lon')), may hold values from -6 to 6
- block_target: int32 [768], P(('lat', 'lon')), may hold values from 0 to 7, as said below
- block_patch: int32 [768], P(('lat', 'lon')), may hold values from 0 to 11
- block_kernel: int32 [768], P(('lat', 'lon')), may hold values from 0 to 15
- encoder_weight: bfloat16 [616, 512], replicated, may hold values from -0.25 to 0.25
- kernels: bfloat16 [16, 128, 128], replicated, may hold values from 0.049804688 to 1
- gain: float32 [512], replicated, may hold values from 0.1 to 1.9
- conv_weight: bfloat16 [3, 3, 512, 512], replicated, may hold values from -0.09375 to 0.09375
- cotangent: bfloat16 [96, 512, 512], P('lat', 'lon'), may hold values from -6 to 6
Outputs:
- conv_out: bfloat16 [96, 512, 512], P('lat', 'lon')
- conv_grad: float32 [3, 3, 512, 512], replicated
- encoder_grad: float32 [616, 512], replicated
- gain_grad: float32 [512], replicated
The draws below stay inside these ranges and needn't reach their ends.
Inputs may be any that keep to these rules, and one draw needn't show every extreme that they name: `block_target`: within one device's 24 blocks no tile is named more than 3 times; in every latitude band one tile is named exactly 3 times by every device of the band.
All inputs are finite; a program needn't handle non-finite values.
Results may differ from the reference program's by a relative error of at most 0.0059.
Values may be sent and summed in bfloat16 or wider, within the bound.
No kernel may reach another device: no remote copies, remote signals or barrier semaphores. Data moves between devices by JAX's collectives and lax.ppermute only.
A program may use at most 192 MiB of HBM per device.

```python
import math
import jax
import jax.numpy as jnp
from jax import lax

CH = 616
D = 512
BLK = 128
PH = 8
PW = 16
NKER = 16
BLOCKS = 24
TH = 24
TW = 64
MOST = 3
NOBS = 98304
NBLK = 768
NLAT = 96
NLON = 512
PATCH = 128
PATCHES = 12
N_LAT = 4
N_LON = 8


def draw_block_target(key, part):
    other_slots = (N_LON - 1) * MOST
    spare_blocks = BLOCKS - MOST

    def one_device(device):
        lat_band = device // N_LON
        hot_key = jax.random.fold_in(jax.random.fold_in(key, 101), lat_band)
        hottest = jax.random.randint(hot_key, (), 0, N_LON)
        own_key = jax.random.fold_in(jax.random.fold_in(key, 202), device)
        first_key, second_key = jax.random.split(own_key)
        others = (hottest + 1 + jnp.arange(other_slots) // MOST) % N_LON
        scores = jax.random.permutation(first_key, other_slots)
        _, chosen = lax.top_k(scores, spare_blocks)
        targets = jnp.concatenate([jnp.full((MOST,), hottest, jnp.int32), others[chosen].astype(jnp.int32)])
        return targets[jax.random.permutation(second_key, BLOCKS)]
    return jax.vmap(one_device)(jnp.arange(NBLK // BLOCKS)).reshape(-1).astype(jnp.int32)


def with_ends(values, key, smallest, largest):
    shape = values.shape
    index_at = [jax.random.randint(jax.random.fold_in(key, axis), (), 0, shape[axis]) for axis in range(len(shape))]
    values = values.at[tuple(index_at)].set(smallest)
    longest = shape.index(max(shape))
    index_at[longest] = (index_at[longest] + 1) % shape[longest]
    return values.at[tuple(index_at)].set(largest)


def block_levels(key, shape, cuts, smallest, top_value):
    level = 1.0
    for position, parts in cuts:
        heights = jax.random.uniform(jax.random.fold_in(jax.random.fold_in(key, 6), position), (parts,), jnp.float32, smallest / len(cuts), top_value / len(cuts))
        level = level * jnp.repeat(jnp.exp(heights), shape[position] // parts).reshape((-1,) + (1,) * (len(shape) - 1 - position))
    return level


def gaussian(key, extent, width, limit, pieces=(), held_as=jnp.bfloat16):
    values = jax.random.normal(key, extent, jnp.float32) * width
    if len(pieces) > 0:
        values = block_levels(key, extent, pieces, -0.22, 0.18) * values
    return jnp.clip(values, min=-limit, max=limit).astype(held_as)


def setup_inputs(seed: int = 0) -> dict:
    seeds = jax.random.split(jax.random.key(seed), 10)
    return {
        "spectra": gaussian(seeds[0], (NOBS, CH), 1.0, 6.0, ((0, 32),)),
        "block_target": draw_block_target(jax.random.fold_in(seeds[9], 71), 0),
        "block_patch": with_ends(jax.random.randint(seeds[2], (NBLK,), 0, PATCHES), jax.random.fold_in(seeds[2], 1), 0, PATCHES - 1).astype(jnp.int32),
        "block_kernel": with_ends(jax.random.randint(seeds[3], (NBLK,), 0, NKER), jax.random.fold_in(seeds[3], 1), 0, NKER - 1).astype(jnp.int32),
        "encoder_weight": gaussian(seeds[4], (CH, D), CH ** -0.5, 0.25),
        "kernels": jnp.clip(jax.random.uniform(seeds[5], (NKER, BLK, PATCH), jnp.float32, 0.049804688, 1.0), 0.049804688, 1.0).astype(jnp.bfloat16),
        "gain": jnp.clip(1.0 + 0.18 * jax.random.normal(seeds[6], (D,), jnp.float32), 0.1, 1.9),
        "conv_weight": gaussian(seeds[7], (3, 3, D, D), (9 * D) ** -0.5, 0.09375),
        "cotangent": gaussian(seeds[8], (NLAT, NLON, D), 1.0, 6.0, ((0, 4), (1, 8))),
    }


def normalise(field, gain):
    meansq = lax.optimization_barrier(jnp.mean(field * field, axis=-1, keepdims=True))
    return field * lax.rsqrt(meansq + 1e-06) * gain

def silu_slope(preact):
    logistic = jax.nn.sigmoid(preact)
    return logistic * (1.0 + preact * (1.0 - logistic))

def widen_global(field):
    beside_all = jnp.concatenate([field[:, -1:], field, field[:, :1]], axis=1)
    return jnp.pad(beside_all, ((1, 1), (0, 0), (0, 0)))

def reference(spectra, block_target, block_patch, block_kernel, encoder_weight, kernels, gain, conv_weight, cotangent):
    block_count = block_target.shape[0]
    preact = jnp.dot(spectra, encoder_weight, preferred_element_type=jnp.float32)
    encoded = jax.nn.silu(preact).astype(jnp.bfloat16).reshape(block_count, BLK, D)
    block_kernels = kernels[block_kernel]
    contribution = jnp.einsum('nbp,nbd->npd', block_kernels.astype(jnp.float32), encoded.astype(jnp.float32))
    owner_device = jnp.arange(block_count, dtype=jnp.int32) // BLOCKS
    lat_band = owner_device // N_LON
    patch_ids = ((lat_band * N_LON + block_target) * PATCHES + block_patch).astype(jnp.int32)
    grid_patches = jnp.zeros((N_LAT * N_LON * PATCHES, PATCH, D), jnp.float32).at[patch_ids].add(contribution)
    spread = grid_patches.reshape(N_LAT, N_LON, TH // PH, TW // PW, PH, PW, D)
    spread = spread.transpose(0, 2, 4, 1, 3, 5, 6).reshape(NLAT, NLON, D)
    normed = normalise(spread, gain).astype(jnp.bfloat16)
    padded = widen_global(normed)
    result_sum = jnp.zeros((NLAT * NLON, D), jnp.float32)
    for row_shift in range(3):
        for col_shift in range(3):
            window = padded[row_shift:row_shift + NLAT, col_shift:col_shift + NLON].reshape(-1, D)
            result_sum = result_sum + jnp.dot(window, conv_weight[row_shift, col_shift], preferred_element_type=jnp.float32)
    conv_out = result_sum.reshape(NLAT, NLON, D).astype(jnp.bfloat16)
    loss_scale = 1.0 / math.sqrt(NLAT * NLON)
    cot_padded = widen_global(cotangent)
    cot_flat = cotangent.reshape(-1, D)
    d_normed = jnp.zeros((NLAT * NLON, D), jnp.float32)
    kernel_grads = []
    for row_shift in range(3):
        for col_shift in range(3):
            back_window = cot_padded[2 - row_shift:2 - row_shift + NLAT, 2 - col_shift:2 - col_shift + NLON].reshape(-1, D)
            d_normed = d_normed + lax.dot_general(back_window, conv_weight[row_shift, col_shift], (((1,), (1,)), ((), ())), preferred_element_type=jnp.float32)
            window = padded[row_shift:row_shift + NLAT, col_shift:col_shift + NLON].reshape(-1, D)
            kernel_grads.append(lax.dot_general(window, cot_flat, (((0,), (0,)), ((), ())), preferred_element_type=jnp.float32))
    conv_grad = jnp.stack(kernel_grads).reshape(3, 3, D, D) * loss_scale
    _, pullback = jax.vjp(normalise, spread, gain)
    d_spread, gain_part = pullback(d_normed.reshape(NLAT, NLON, D))
    gain_grad = gain_part * loss_scale
    d_spread = d_spread.astype(jnp.bfloat16)
    d_patches = d_spread.reshape(N_LAT, TH // PH, PH, N_LON, TW // PW, PW, D)
    d_patches = d_patches.transpose(0, 3, 1, 4, 2, 5, 6).reshape(-1, PATCH, D)
    block_dpatch = d_patches[patch_ids]
    d_rows = jnp.einsum('nbp,npd->nbd', block_kernels.astype(jnp.float32), block_dpatch.astype(jnp.float32)).astype(jnp.bfloat16)
    d_preact = (d_rows.reshape(-1, D).astype(jnp.float32) * silu_slope(preact)).astype(jnp.bfloat16)
    encoder_grad = lax.dot_general(spectra, d_preact, (((0,), (0,)), ((), ())), preferred_element_type=jnp.float32) * loss_scale
    return (conv_out, conv_grad, encoder_grad, gain_grad)
```

```python
import math

import jax
import jax.numpy as jnp
from jax import lax
from jax.experimental import pallas as pl
from jax.experimental.pallas import tpu as pltpu
from jax.sharding import PartitionSpec as P

PH = 8
PW = 16
MOST = 3
EPS = 1e-06
AXES = ("lat", "lon")
VMEM_LIMIT = 56 * 1024 * 1024


def bits_of(count):
    assert count & (count - 1) == 0
    return [1 << i for i in range(count.bit_length() - 1)]


def parity(value, mask):
    out = jnp.zeros((), jnp.int32)
    while mask:
        low = mask & -mask
        out = out ^ ((value & low) != 0).astype(jnp.int32)
        mask ^= low
    return out


def exchange(value, lats, lons, move):
    pairs = []
    for a in range(lats):
        for b in range(lons):
            c, d = move(a, b)
            pairs.append((a * lons + b, c * lons + d))
    return lax.ppermute(value, AXES, pairs)


def stage_plan(lats, lons):
    lat_bits, lon_bits = bits_of(lats), bits_of(lons)
    first = lat_bits[:1]
    lat_rest = lat_bits[1:]
    low, high = lon_bits[:1], lon_bits[1:]
    plan = [(((m, 0), (m, 0)), ((m, 0), (m, 0))) for m in first]
    ab = [(m, 0) for m in lat_rest] + [(0, m) for m in low]
    ba = [(0, m) for m in low] + [(m, 0) for m in lat_rest]
    plan += [((p, q), (p, q)) for p, q in zip(ab, ba)]
    if len(high) == 2:
        one, two = high
        plan += [(((0, one),) * 2, ((0, one | two),) * 2), (((0, one | two),) * 2, ((0, two),) * 2)]
    else:
        plan += [(((0, m),) * 2, ((0, m),) * 2) for m in high]
    return plan


def kept_half(masks, lat, lon):
    even = parity(lat, masks[0][0]) ^ parity(lon, masks[0][1])
    odd = parity(lat, masks[1][0]) ^ parity(lon, masks[1][1])
    return jnp.where((lat & 1) == 0, even, odd)


def step(value, steps, lats, lons):
    return exchange(value, lats, lons, lambda a, b: (a ^ steps[a & 1][0], b ^ steps[a & 1][1]))


def pick(value, half):
    pair = value.reshape(2, value.shape[0] // 2, value.shape[1])
    return lax.dynamic_index_in_dim(pair, half, 0, keepdims=False)


def split_sum(keep, came, half):
    away = pick(keep, 1 - half) + pick(came, 1 - half).astype(jnp.float32)
    stay = pick(keep, half) + pick(came, half).astype(jnp.float32)
    return away.astype(jnp.bfloat16), stay


def padded_2(shard, sides, width, wrap):
    for axis, dim in sides:
        size, length = (lax.axis_size(axis), shard.shape[dim])
        up = [(i, (i + 1) % size) for i in range(size if wrap else size - 1)]
        down = [(j, i) for i, j in up]
        last = lax.slice_in_dim(shard, length - width, length, axis=dim)
        leading = lax.slice_in_dim(shard, 0, width, axis=dim)
        before = lax.ppermute(last, axis, up)
        after = lax.ppermute(leading, axis, down)
        shard = jnp.concatenate([before, shard, after], axis=dim)
    return shard


def widen(field):
    beside_all = padded_2(field, (("lon", 1),), 1, True)
    return padded_2(beside_all, (("lat", 0),), 1, False)


def to_patches(tile):
    rows, cols, width = tile.shape
    shaped = tile.reshape(rows // PH, PH, cols // PW, PW, width)
    return shaped.transpose(0, 2, 1, 3, 4).reshape(-1, width)


def whole(shape):
    zeros = (0,) * len(shape)
    return pl.BlockSpec(shape, lambda *_: zeros)


def call(body, scalars, ins, outs, name, grid=(1,), in_specs=None, out_specs=None, scratch=(), alias=None):
    return pl.pallas_call(
        body,
        out_shape=outs,
        grid_spec=pltpu.PrefetchScalarGridSpec(
            num_scalar_prefetch=1,
            grid=grid,
            in_specs=in_specs or [whole(a.shape) for a in ins],
            out_specs=out_specs or [whole(o.shape) for o in outs],
            scratch_shapes=list(scratch),
        ),
        input_output_aliases=alias or {},
        compiler_params=pltpu.CompilerParams(vmem_limit_bytes=VMEM_LIMIT),
        name=name,
    )(scalars, *ins)


def shape_of(shape, dtype):
    return jax.ShapeDtypeStruct(shape, dtype)


def nt(left, right):
    return lax.dot_general(left, right, (((1,), (1,)), ((), ())), preferred_element_type=jnp.float32)


def lanes(at, size):
    return pl.ds(pl.multiple_of(at * size, size), size)


def pack(spectra_t, source, count, rows):
    channels = spectra_t.shape[0]

    def body(src, full, *outs):
        for k in range(count):
            for j in range(MOST):
                outs[k][:, j * rows : (j + 1) * rows] = full[:, lanes(src[k * MOST + j], rows)]

    outs = [shape_of((channels, MOST * rows), spectra_t.dtype)] * count
    return call(body, source, [spectra_t], outs, "pack_blocks")


def forward(meta, arrived, weight_t, kernels, gain_col):
    count = len(arrived)
    kernel_count, rows, cells = kernels.shape
    width = weight_t.shape[0]

    def make(patches):
        def body(meta_ref, *refs):
            xs = refs[:count]
            w, kern, g, normed, spread, slope = refs[count:]
            spread[...] = jnp.zeros_like(spread)
            for k in range(count):
                pre = jnp.dot(w[...], xs[k][...], preferred_element_type=jnp.float32)
                s = jax.nn.sigmoid(pre)
                slope[k] = (s * (1.0 + pre * (1.0 - s))).astype(jnp.bfloat16)
                enc = (pre * s).astype(jnp.bfloat16)
                for j in range(MOST):
                    code = meta_ref[k * MOST + j]

                    @pl.when(code >= 0)
                    def _():
                        spread[code // kernel_count] += jnp.dot(
                            enc[:, j * rows : (j + 1) * rows],
                            kern[code % kernel_count],
                            preferred_element_type=jnp.float32,
                        )

            for q in range(patches):
                cell = spread[q]
                r = lax.rsqrt(jnp.mean(cell * cell, axis=0, keepdims=True) + EPS)
                normed[:, q * cells : (q + 1) * cells] = (cell * r * g[...]).astype(jnp.bfloat16)

        return body

    def run(patches):
        outs = [
            shape_of((width, patches * cells), jnp.bfloat16),
            shape_of((patches, width, cells), jnp.float32),
            shape_of((count, width, MOST * rows), jnp.bfloat16),
        ]
        ins = [*arrived, weight_t, kernels, gain_col]
        return call(make(patches), meta, ins, outs, "encode_spread_norm")

    return run


def backward(meta, arrived, kernels_t, gain_col, spread, slope, d_normed_t):
    count = len(arrived)
    kernel_count, cells, rows = kernels_t.shape
    patches, width, _ = spread.shape
    channels = arrived[0].shape[0]

    def body(meta_ref, *refs):
        xs = refs[:count]
        kern, g, spr, slo, dn, enc_grad, gain_grad, dsp, dpre = refs[count:]
        total = jnp.zeros((width, cells), jnp.float32)
        for q in range(patches):
            cell = spr[q]
            d = dn[:, q * cells : (q + 1) * cells]
            r = lax.rsqrt(jnp.mean(cell * cell, axis=0, keepdims=True) + EPS)
            unit = cell * r
            total = total + d * unit
            dg = d * g[...]
            inner = jnp.mean(dg * unit, axis=0, keepdims=True)
            dsp[q] = ((dg - unit * inner) * r).astype(jnp.bfloat16)
        gain_grad[...] = total
        for k in range(count):
            for j in range(MOST):
                code = meta_ref[k * MOST + j]
                span = slice(j * rows, (j + 1) * rows)

                @pl.when(code >= 0)
                def _():
                    drow = jnp.dot(
                        dsp[code // kernel_count],
                        kern[code % kernel_count],
                        preferred_element_type=jnp.float32,
                    ).astype(jnp.bfloat16)
                    dpre[:, span] = (
                        drow.astype(jnp.float32) * slo[k, :, span].astype(jnp.float32)
                    ).astype(jnp.bfloat16)

                @pl.when(code < 0)
                def _():
                    dpre[:, span] = jnp.zeros((width, rows), jnp.bfloat16)

            part = nt(xs[k][...], dpre[...])
            if k == 0:
                enc_grad[...] = part
            else:
                enc_grad[...] += part

    ins = [*arrived, kernels_t, gain_col, spread, slope, d_normed_t]
    outs = [shape_of((channels, width), jnp.float32), shape_of((width, cells), jnp.float32)]
    scratch = [
        pltpu.VMEM((patches, width, cells), jnp.bfloat16),
        pltpu.VMEM((width, MOST * rows), jnp.bfloat16),
    ]
    return call(body, meta, ins, outs, "unnorm_gather_encode_grad", scratch=scratch)


def conv_half(half, normed_t, windows, dtype, name):
    taps, cells, width = windows.shape
    unit = width // 2

    def body(half_ref, left, right, out):
        number = half_ref[0] * taps + pl.program_id(0)
        rows = left[lanes(number % 2, unit)]
        out[...] = jnp.dot(rows, right[0], preferred_element_type=jnp.float32).astype(dtype)

    return call(
        body,
        half.reshape(1),
        [normed_t, windows],
        [shape_of((taps * unit, width), dtype)],
        name,
        grid=(taps,),
        in_specs=[
            whole(normed_t.shape),
            pl.BlockSpec((1, cells, width), lambda i, h: ((h[0] * taps + i) // 2, 0, 0)),
        ],
        out_specs=[pl.BlockSpec((unit, width), lambda i, h: (i, 0))],
    )[0]


def place(half, pieces, rows, scale, name, into=None):
    count, full, width = pieces.shape

    def body(half_ref, piece, *refs):
        refs[-1][...] = piece[0, :rows].astype(jnp.float32) * scale

    specs = [pl.BlockSpec((1, full, width), lambda i, h: (i, 0, 0))]
    ins = [pieces]
    if into is not None:
        ins.append(into)
        specs.append(pl.BlockSpec(memory_space=pl.ANY))
    return call(
        body,
        half.reshape(1),
        ins,
        [shape_of((2 * count * rows, width), jnp.float32)],
        name,
        grid=(count,),
        in_specs=specs,
        out_specs=[pl.BlockSpec((rows, width), lambda i, h: (h[0] * count + i, 0))],
        alias=None if into is None else {2: 0},
    )[0]


def shards(
    spectra,
    block_target,
    block_patch,
    block_kernel,
    encoder_weight,
    kernels,
    gain,
    conv_weight,
    cotangent,
):
    lons = lax.axis_size("lon")
    lats = lax.axis_size("lat")
    lon = lax.axis_index("lon")
    blocks = block_target.shape[0]
    kernel_count, block_rows, _ = kernels.shape
    channels = spectra.shape[1]
    width = encoder_weight.shape[1]
    tile_rows, tile_cols = (cotangent.shape[0], cotangent.shape[1])
    loss_scale = 1.0 / math.sqrt(tile_rows * lats * tile_cols * lons)
    cells = tile_rows * tile_cols

    order = lon ^ jnp.arange(lons, dtype=jnp.int32)
    hit = (block_target[:, None] == order[None, :]).astype(jnp.int32)
    rank = jnp.cumsum(hit, axis=0) - hit
    chosen = hit[:, :, None] * (rank[:, :, None] == jnp.arange(MOST)[None, None, :]).astype(jnp.int32)
    number = jnp.arange(blocks, dtype=jnp.int32)
    source = jnp.sum(chosen * number[:, None, None], axis=0).reshape(-1)
    code = block_patch * kernel_count + block_kernel + 1
    codes = jnp.sum(chosen * code[:, None, None], axis=0) - 1
    spectra_t = spectra.T
    packed = pack(spectra_t, source, lons, block_rows)

    cot_padded = widen(cotangent)

    by_tile = jnp.sum(
        jnp.where((order[None, :] == jnp.arange(lons)[:, None])[:, :, None], codes[None], 0), axis=1
    )
    came = lax.all_to_all(by_tile, "lon", 0, 0, tiled=True)
    meta = jnp.sum(
        jnp.where((order[:, None] == jnp.arange(lons)[None, :])[:, :, None], came[None], 0), axis=1
    ).reshape(-1)

    arrived = [packed[0]] + [
        exchange(packed[k], lats, lons, lambda a, b, k=k: (a, b ^ k)) for k in range(1, lons)
    ]

    patches = tile_rows // PH * (tile_cols // PW)
    gain_col = gain.reshape(width, 1)
    normed_t, spread, slope = forward(
        meta, arrived, encoder_weight.T, kernels, gain_col
    )(patches)

    windows = jnp.stack(
        [
            to_patches(cot_padded[2 - a : 2 - a + tile_rows, 2 - b : 2 - b + tile_cols])
            for a in range(3)
            for b in range(3)
        ]
    )
    d_normed_t = jnp.zeros((width, cells), jnp.float32)
    for tap in range(9):
        d_normed_t = d_normed_t + nt(conv_weight[tap // 3, tap % 3], windows[tap])

    plan = stage_plan(lats, lons)
    lat = lax.axis_index("lat")
    halves = [kept_half(masks, lat, lon) for _, masks in plan]
    core = halves[0]
    away = conv_half(1 - core, normed_t, windows, jnp.bfloat16, "conv_grad_away")
    keep = conv_half(core, normed_t, windows, jnp.float32, "conv_grad_keep")
    came = step(away, plan[0][0], lats, lons)

    encoder_part, gain_part = backward(
        meta, arrived, kernels.transpose(0, 2, 1), gain_col, spread, slope, d_normed_t
    )
    half_channels = -(-channels // 2)
    unit = 4 * lats * lons
    small_rows = -(-(half_channels + 1) // unit) * unit
    gain_part = jnp.sum(gain_part, axis=1)[None]
    small = jnp.concatenate(
        [encoder_part, jnp.zeros((2 * half_channels - channels, width), jnp.float32)]
    ).reshape(2, half_channels, width)
    small = jnp.concatenate(
        [
            small,
            jnp.broadcast_to(gain_part, (2, 1, width)),
            jnp.zeros((2, small_rows - half_channels - 1, width), jnp.float32),
        ],
        axis=1,
    ).reshape(2 * small_rows, width)
    small_keep = pick(small, core)
    small_came = step(pick(small, 1 - core).astype(jnp.bfloat16), plan[0][0], lats, lons)

    apart = len(plan) - 2
    for n in range(1, apart):
        away, keep = split_sum(keep, came, halves[n])
        came = step(away, plan[n][0], lats, lons)
        away, small_keep = split_sum(small_keep, small_came, halves[n])
        small_came = step(away, plan[n][0], lats, lons)
    big = keep.shape[0]
    keep = jnp.concatenate([keep, small_keep])
    came = jnp.concatenate([came, small_came])
    for n in range(apart, len(plan)):
        away, keep = split_sum(keep, came, halves[n])
        came = step(away, plan[n][0], lats, lons)
    part = (keep + came.astype(jnp.float32)).astype(jnp.bfloat16)
    for n in range(len(plan) - 1, 0, -1):
        other = step(part, plan[n][0], lats, lons)
        part = jnp.where(
            halves[n] == 0, jnp.concatenate([part, other]), jnp.concatenate([other, part])
        )
    pieces = part.reshape(-1, big + small_came.shape[0], width)
    others = step(pieces, plan[0][0], lats, lons)
    conv_total = place(core, pieces, big, loss_scale, "own_half")
    conv_total = place(1 - core, others, big, loss_scale, "other_half", conv_total)
    mine = pieces[:, big:].reshape(small_rows, width)
    theirs = others[:, big:].reshape(small_rows, width)
    gain_total = mine[half_channels].astype(jnp.float32) * loss_scale
    mine, theirs = mine[:half_channels], theirs[:half_channels]
    encoder_total = jnp.where(
        core == 0, jnp.concatenate([mine, theirs]), jnp.concatenate([theirs, mine])
    )[:channels].astype(jnp.float32) * loss_scale

    normed = normed_t.reshape(width, tile_rows // PH, tile_cols // PW, PH, PW)
    normed = normed.transpose(1, 3, 2, 4, 0).reshape(tile_rows, tile_cols, width)
    padded = widen(normed)
    result_sum = jnp.zeros((cells, width), jnp.float32)
    for a in range(3):
        for b in range(3):
            window = padded[a : a + tile_rows, b : b + tile_cols].reshape(-1, width)
            result_sum = result_sum + jnp.dot(
                window, conv_weight[a, b], preferred_element_type=jnp.float32
            )
    conv_out = result_sum.reshape(tile_rows, tile_cols, width).astype(jnp.bfloat16)
    return (conv_out, conv_total.reshape(3, 3, width, width), encoder_total, gain_total)


def solution(mesh):
    placed = (
        P(("lat", "lon"), None),
        P(("lat", "lon")),
        P(("lat", "lon")),
        P(("lat", "lon")),
        P(),
        P(),
        P(),
        P(),
        P("lat", "lon", None),
    )
    return jax.shard_map(
        shards,
        mesh=mesh,
        in_specs=placed,
        out_specs=(P("lat", "lon", None), P(), P(), P()),
        check_vma=False,
    )
```

```python
import math

import jax
import jax.numpy as jnp
from jax import lax
from jax.experimental import pallas as pl
from jax.experimental.pallas import tpu as pltpu
from jax.sharding import PartitionSpec as P

PH = 8
PW = 16
MOST = 3
EPS = 1e-06
LANES = 128
AXES = ("lat", "lon")
VMEM_LIMIT = 56 * 1024 * 1024


def bits_of(count):
    assert count & (count - 1) == 0
    return [1 << i for i in range(count.bit_length() - 1)]


def parity(value, mask):
    out = jnp.zeros((), jnp.int32)
    while mask:
        low = mask & -mask
        out = out ^ ((value & low) != 0).astype(jnp.int32)
        mask ^= low
    return out


def exchange(value, lats, lons, move):
    pairs = []
    for a in range(lats):
        for b in range(lons):
            c, d = move(a, b)
            pairs.append((a * lons + b, c * lons + d))
    return lax.ppermute(value, AXES, pairs)


def stage_plan(lats, lons):
    lat_bits, lon_bits = bits_of(lats), bits_of(lons)
    first = lat_bits[:1]
    lat_rest = lat_bits[1:]
    low, high = lon_bits[:1], lon_bits[1:]
    plan = [(((m, 0), (m, 0)), ((m, 0), (m, 0))) for m in first]
    ab = [(m, 0) for m in lat_rest] + [(0, m) for m in low]
    ba = [(0, m) for m in low] + [(m, 0) for m in lat_rest]
    plan += [((p, q), (p, q)) for p, q in zip(ab, ba)]
    if len(high) == 2:
        one, two = high
        plan += [(((0, one),) * 2, ((0, one | two),) * 2), (((0, one | two),) * 2, ((0, two),) * 2)]
    else:
        plan += [(((0, m),) * 2, ((0, m),) * 2) for m in high]
    return plan


def kept_half(masks, lat, lon):
    even = parity(lat, masks[0][0]) ^ parity(lon, masks[0][1])
    odd = parity(lat, masks[1][0]) ^ parity(lon, masks[1][1])
    return jnp.where((lat & 1) == 0, even, odd)


def step(value, steps, lats, lons):
    return exchange(value, lats, lons, lambda a, b: (a ^ steps[a & 1][0], b ^ steps[a & 1][1]))


def pick(value, half):
    pair = value.reshape(2, value.shape[0] // 2, value.shape[1])
    return lax.dynamic_index_in_dim(pair, half, 0, keepdims=False)


def split_sum(keep, came, half):
    away = pick(keep, 1 - half) + pick(came, 1 - half).astype(jnp.float32)
    stay = pick(keep, half) + pick(came, half).astype(jnp.float32)
    return away.astype(jnp.bfloat16), stay


def padded_2(shard, sides, width, wrap):
    for axis, dim in sides:
        size, length = (lax.axis_size(axis), shard.shape[dim])
        up = [(i, (i + 1) % size) for i in range(size if wrap else size - 1)]
        down = [(j, i) for i, j in up]
        last = lax.slice_in_dim(shard, length - width, length, axis=dim)
        leading = lax.slice_in_dim(shard, 0, width, axis=dim)
        before = lax.ppermute(last, axis, up)
        after = lax.ppermute(leading, axis, down)
        shard = jnp.concatenate([before, shard, after], axis=dim)
    return shard


def widen(field):
    beside_all = padded_2(field, (("lon", 1),), 1, True)
    return padded_2(beside_all, (("lat", 0),), 1, False)


def to_patches(tile):
    rows, cols, width = tile.shape
    shaped = tile.reshape(rows // PH, PH, cols // PW, PW, width)
    return shaped.transpose(0, 2, 1, 3, 4).reshape(-1, width)


def whole(shape):
    zeros = (0,) * len(shape)
    return pl.BlockSpec(shape, lambda *_: zeros)


def call(body, scalars, ins, outs, name, grid=(1,), in_specs=None, out_specs=None, scratch=(), alias=None):
    return pl.pallas_call(
        body,
        out_shape=outs,
        grid_spec=pltpu.PrefetchScalarGridSpec(
            num_scalar_prefetch=1,
            grid=grid,
            in_specs=in_specs or [whole(a.shape) for a in ins],
            out_specs=out_specs or [whole(o.shape) for o in outs],
            scratch_shapes=list(scratch),
        ),
        input_output_aliases=alias or {},
        compiler_params=pltpu.CompilerParams(vmem_limit_bytes=VMEM_LIMIT),
        name=name,
    )(scalars, *ins)


def shape_of(shape, dtype):
    return jax.ShapeDtypeStruct(shape, dtype)


def nt(left, right):
    return lax.dot_general(left, right, (((1,), (1,)), ((), ())), preferred_element_type=jnp.float32)


def lanes(at, size):
    return pl.ds(pl.multiple_of(at * size, size), size)


def pack(spectra_t, source, count, rows):
    channels = spectra_t.shape[0]

    def body(src, full, *outs):
        for k in range(count):
            for j in range(MOST):
                outs[k][:, j * rows : (j + 1) * rows] = full[:, lanes(src[k * MOST + j], rows)]

    outs = [shape_of((channels, MOST * rows), spectra_t.dtype)] * count
    return call(body, source, [spectra_t], outs, "pack_blocks")


def spread_blocks(meta, first, arrived, weight_t, kernels, gain_col, before, patches, last):
    count = len(arrived)
    kernel_count, rows, cells = kernels.shape
    width = weight_t.shape[0]

    def body(meta_ref, *refs):
        xs = refs[:count]
        w, kern, g = refs[count : count + 3]
        spread, slope, *rest = refs[count + 3 + (before is not None) :]
        if before is None:
            spread[...] = jnp.zeros_like(spread)
        else:
            spread[...] = refs[count + 3][...]
        for k in range(count):
            pre = jnp.dot(w[...], xs[k][...], preferred_element_type=jnp.float32)
            s = jax.nn.sigmoid(pre)
            slope[k] = (s * (1.0 + pre * (1.0 - s))).astype(jnp.bfloat16)
            enc = (pre * s).astype(jnp.bfloat16)
            for j in range(MOST):
                code = meta_ref[(first + k) * MOST + j]

                @pl.when(code >= 0)
                def _():
                    spread[code // kernel_count] += jnp.dot(
                        enc[:, j * rows : (j + 1) * rows],
                        kern[code % kernel_count],
                        preferred_element_type=jnp.float32,
                    )

        if last:
            for q in range(patches):
                cell = spread[q]
                r = lax.rsqrt(jnp.mean(cell * cell, axis=0, keepdims=True) + EPS)
                rest[0][:, q * cells : (q + 1) * cells] = (cell * r * g[...]).astype(jnp.bfloat16)

    outs = [
        shape_of((patches, width, cells), jnp.float32),
        shape_of((count, width, MOST * rows), jnp.bfloat16),
    ]
    if last:
        outs.append(shape_of((width, patches * cells), jnp.bfloat16))
    ins = [*arrived, weight_t, kernels, gain_col] + ([] if before is None else [before])
    return call(body, meta, ins, outs, "encode_spread_norm" if last else "encode_spread")


def backward(meta, arrived, kernels_t, gain_col, spread, slopes, d_normed_t):
    count = len(arrived)
    groups = len(slopes)
    place_of = [(n, k) for n, one in enumerate(slopes) for k in range(one.shape[0])]
    kernel_count, cells, rows = kernels_t.shape
    patches, width, _ = spread.shape
    channels = arrived[0].shape[0]

    def body(meta_ref, *refs):
        xs = refs[:count]
        slos = refs[count : count + groups]
        kern, g, spr, dn, out, dsp, dpre = refs[count + groups :]
        total = jnp.zeros((width, 1), jnp.float32)
        for q in range(patches):
            cell = spr[q]
            d = dn[:, q * cells : (q + 1) * cells]
            r = lax.rsqrt(jnp.mean(cell * cell, axis=0, keepdims=True) + EPS)
            unit = cell * r
            total = total + jnp.sum(d * unit, axis=1, keepdims=True)
            dg = d * g[...]
            inner = jnp.mean(dg * unit, axis=0, keepdims=True)
            dsp[q] = ((dg - unit * inner) * r).astype(jnp.bfloat16)
        out[...] = jnp.zeros_like(out)
        out[:, channels : channels + 1] = total
        for k in range(count):
            for j in range(MOST):
                code = meta_ref[k * MOST + j]
                span = slice(j * rows, (j + 1) * rows)

                @pl.when(code >= 0)
                def _():
                    drow = jnp.dot(
                        dsp[code // kernel_count],
                        kern[code % kernel_count],
                        preferred_element_type=jnp.float32,
                    ).astype(jnp.bfloat16)
                    dpre[:, span] = (
                        drow.astype(jnp.float32) * slos[place_of[k][0]][place_of[k][1], :, span].astype(jnp.float32)
                    ).astype(jnp.bfloat16)

                @pl.when(code < 0)
                def _():
                    dpre[:, span] = jnp.zeros((width, rows), jnp.bfloat16)

            out[:, :channels] += nt(dpre[...], xs[k][...])

    ins = [*arrived, *slopes, kernels_t, gain_col, spread, d_normed_t]
    outs = [shape_of((width, (channels // LANES + 1) * LANES), jnp.float32)]
    scratch = [
        pltpu.VMEM((patches, width, cells), jnp.bfloat16),
        pltpu.VMEM((width, MOST * rows), jnp.bfloat16),
    ]
    return call(body, meta, ins, outs, "unnorm_gather_encode_grad", scratch=scratch)[0]


def place(half, part, taps, lane, scale, name, into=None):
    rows = part.shape[0]
    unit = rows // 4

    def body(half_ref, piece, *refs):
        for t in range(taps):
            refs[-1][t] = piece[:, t * lane : (t + 1) * lane].astype(jnp.float32) * scale

    specs = [pl.BlockSpec((unit, part.shape[1]), lambda i, h: (i, 0))]
    ins = [part]
    if into is not None:
        ins.append(into)
        specs.append(pl.BlockSpec(memory_space=pl.ANY))
    return call(
        body,
        half.reshape(1),
        ins,
        [shape_of((taps, 2 * rows, lane), jnp.float32)],
        name,
        grid=(4,),
        in_specs=specs,
        out_specs=[pl.BlockSpec((taps, unit, lane), lambda i, h: (0, h[0] * 4 + i, 0))],
        alias=None if into is None else {2: 0},
    )[0]


def shards(
    spectra,
    block_target,
    block_patch,
    block_kernel,
    encoder_weight,
    kernels,
    gain,
    conv_weight,
    cotangent,
):
    lons = lax.axis_size("lon")
    lats = lax.axis_size("lat")
    lon = lax.axis_index("lon")
    blocks = block_target.shape[0]
    kernel_count, block_rows, _ = kernels.shape
    channels = spectra.shape[1]
    width = encoder_weight.shape[1]
    tile_rows, tile_cols = (cotangent.shape[0], cotangent.shape[1])
    loss_scale = 1.0 / math.sqrt(tile_rows * lats * tile_cols * lons)
    cells = tile_rows * tile_cols

    cot_beside = padded_2(cotangent, (("lon", 1),), 1, True)
    order = lon ^ jnp.arange(lons, dtype=jnp.int32)
    hit = (block_target[:, None] == order[None, :]).astype(jnp.int32)
    rank = jnp.cumsum(hit, axis=0) - hit
    chosen = hit[:, :, None] * (rank[:, :, None] == jnp.arange(MOST)[None, None, :]).astype(jnp.int32)
    number = jnp.arange(blocks, dtype=jnp.int32)
    source = jnp.sum(chosen * number[:, None, None], axis=0).reshape(-1)
    code = block_patch * kernel_count + block_kernel + 1
    codes = jnp.sum(chosen * code[:, None, None], axis=0) - 1
    spectra_t = spectra.T
    source, cot_beside = lax.optimization_barrier((source, cot_beside))
    packed = pack(spectra_t, source, lons, block_rows)
    cot_padded = padded_2(cot_beside, (("lat", 0),), 1, False)

    by_tile = jnp.sum(
        jnp.where((order[None, :] == jnp.arange(lons)[:, None])[:, :, None], codes[None], 0), axis=1
    )
    came = lax.all_to_all(by_tile, "lon", 0, 0, tiled=True)
    meta = jnp.sum(
        jnp.where((order[:, None] == jnp.arange(lons)[None, :])[:, :, None], came[None], 0), axis=1
    ).reshape(-1)

    sent = {}
    for k in list(range(lons - 1, 0, -1)):
        sent[k] = exchange(packed[k], lats, lons, lambda a, b, k=k: (a, b ^ k))
    arrived = [packed[0]] + [sent[k] for k in range(1, lons)]

    patches = tile_rows // PH * (tile_cols // PW)
    gain_col = gain.reshape(width, 1)
    weight_t = encoder_weight.T
    cut = lons - lons // 4
    spread, slope_a = spread_blocks(
        meta, 0, arrived[:cut], weight_t, kernels, gain_col, None, patches, False
    )
    spread, slope_b, normed_t = spread_blocks(
        meta, cut, arrived[cut:], weight_t, kernels, gain_col, spread, patches, True
    )

    windows = jnp.concatenate(
        [
            to_patches(cot_padded[2 - a : 2 - a + tile_rows, 2 - b : 2 - b + tile_cols])
            for a in range(3)
            for b in range(3)
        ],
        axis=1,
    )
    taps = 9
    weight_all = conv_weight.reshape(taps, width, width).transpose(1, 0, 2).reshape(width, -1)
    d_normed_t = nt(weight_all, windows)

    plan = stage_plan(lats, lons)
    lat = lax.axis_index("lat")
    halves = [kept_half(masks, lat, lon) for _, masks in plan]
    core = halves[0]
    away = jnp.dot(
        pick(normed_t, 1 - core), windows, preferred_element_type=jnp.float32
    ).astype(jnp.bfloat16)
    keep = jnp.dot(pick(normed_t, core), windows, preferred_element_type=jnp.float32)
    came = step(away, plan[0][0], lats, lons)

    small = backward(
        meta, arrived, kernels.transpose(0, 2, 1), gain_col, spread, (slope_a, slope_b), d_normed_t
    )
    small_keep = pick(small, core)
    small_came = step(pick(small, 1 - core).astype(jnp.bfloat16), plan[0][0], lats, lons)

    apart = len(plan) - 2
    for n in range(1, apart):
        away, keep = split_sum(keep, came, halves[n])
        came = step(away, plan[n][0], lats, lons)
        away, small_keep = split_sum(small_keep, small_came, halves[n])
        small_came = step(away, plan[n][0], lats, lons)
    wide = taps * width
    keep = jnp.concatenate([keep, small_keep], axis=1)
    came = jnp.concatenate([came, small_came], axis=1)
    for n in range(apart, len(plan)):
        away, keep = split_sum(keep, came, halves[n])
        came = step(away, plan[n][0], lats, lons)
    part = (keep + came.astype(jnp.float32)).astype(jnp.bfloat16)
    for n in range(len(plan) - 1, 0, -1):
        other = step(part, plan[n][0], lats, lons)
        part = jnp.where(
            halves[n] == 0, jnp.concatenate([part, other]), jnp.concatenate([other, part])
        )
    others = step(part, plan[0][0], lats, lons)
    conv_total = place(core, part, taps, width, loss_scale, "own_half")
    conv_total = place(1 - core, others, taps, width, loss_scale, "other_half", conv_total)
    mine, theirs = part[:, wide:], others[:, wide:]
    small = jnp.where(
        core == 0, jnp.concatenate([mine, theirs]), jnp.concatenate([theirs, mine])
    ).astype(jnp.float32) * loss_scale
    gain_total = small[:, channels]
    encoder_total = small[:, :channels].T

    normed = normed_t.reshape(width, tile_rows // PH, tile_cols // PW, PH, PW)
    normed = normed.transpose(1, 3, 2, 4, 0).reshape(tile_rows, tile_cols, width)
    padded = widen(normed)
    result_sum = jnp.zeros((cells, width), jnp.float32)
    for a in range(3):
        for b in range(3):
            window = padded[a : a + tile_rows, b : b + tile_cols].reshape(-1, width)
            result_sum = result_sum + jnp.dot(
                window, conv_weight[a, b], preferred_element_type=jnp.float32
            )
    conv_out = result_sum.reshape(tile_rows, tile_cols, width).astype(jnp.bfloat16)
    return (conv_out, conv_total.reshape(3, 3, width, width), encoder_total, gain_total)


def solution(mesh):
    placed = (
        P(("lat", "lon"), None),
        P(("lat", "lon")),
        P(("lat", "lon")),
        P(("lat", "lon")),
        P(),
        P(),
        P(),
        P(),
        P("lat", "lon", None),
    )
    return jax.shard_map(
        shards,
        mesh=mesh,
        in_specs=placed,
        out_specs=(P("lat", "lon", None), P(), P(), P()),
        check_vma=False,
    )
```

```python
import math

import jax
import jax.numpy as jnp
from jax import lax
from jax.experimental import pallas as pl
from jax.experimental.pallas import tpu as pltpu
from jax.sharding import PartitionSpec as P


PH = 8
PW = 16
MOST = 3
EPS = 1e-06
LANES = 128
AXES = ("lat", "lon")
VMEM_LIMIT = 56 * 1024 * 1024


def bits_of(count):
    assert count & (count - 1) == 0
    return [1 << i for i in range(count.bit_length() - 1)]


def parity(value, mask):
    out = jnp.zeros((), jnp.int32)
    while mask:
        low = mask & -mask
        out = out ^ ((value & low) != 0).astype(jnp.int32)
        mask ^= low
    return out


def exchange(value, lats, lons, move):
    pairs = []
    for a in range(lats):
        for b in range(lons):
            c, d = move(a, b)
            pairs.append((a * lons + b, c * lons + d))
    return lax.ppermute(value, AXES, pairs)


def stage_plan(lats, lons):
    lat_bits, lon_bits = bits_of(lats), bits_of(lons)
    first = lat_bits[:1]
    lat_rest = lat_bits[1:]
    low, high = lon_bits[:1], lon_bits[1:]
    plan = [(((m, 0), (m, 0)), ((m, 0), (m, 0))) for m in first]
    ab = [(m, 0) for m in lat_rest] + [(0, m) for m in low]
    ba = [(0, m) for m in low] + [(m, 0) for m in lat_rest]
    plan += [((p, q), (p, q)) for p, q in zip(ab, ba)]
    if len(high) == 2:
        one, two = high
        plan += [(((0, one),) * 2, ((0, one | two),) * 2), (((0, one | two),) * 2, ((0, two),) * 2)]
    else:
        plan += [(((0, m),) * 2, ((0, m),) * 2) for m in high]
    return plan


def kept_half(masks, lat, lon):
    even = parity(lat, masks[0][0]) ^ parity(lon, masks[0][1])
    odd = parity(lat, masks[1][0]) ^ parity(lon, masks[1][1])
    return jnp.where((lat & 1) == 0, even, odd)


def step(value, steps, lats, lons):
    return exchange(value, lats, lons, lambda a, b: (a ^ steps[a & 1][0], b ^ steps[a & 1][1]))


def pick(value, half):
    pair = value.reshape(2, value.shape[0] // 2, value.shape[1])
    return lax.dynamic_index_in_dim(pair, half, 0, keepdims=False)


def split_sum(keep, came, half):
    away = pick(keep, 1 - half) + pick(came, 1 - half).astype(jnp.float32)
    stay = pick(keep, half) + pick(came, half).astype(jnp.float32)
    return away.astype(jnp.bfloat16), stay


def padded_2(shard, sides, width, wrap):
    for axis, dim in sides:
        size, length = (lax.axis_size(axis), shard.shape[dim])
        up = [(i, (i + 1) % size) for i in range(size if wrap else size - 1)]
        down = [(j, i) for i, j in up]
        last = lax.slice_in_dim(shard, length - width, length, axis=dim)
        leading = lax.slice_in_dim(shard, 0, width, axis=dim)
        before = lax.ppermute(last, axis, up)
        after = lax.ppermute(leading, axis, down)
        shard = jnp.concatenate([before, shard, after], axis=dim)
    return shard


def widen(field):
    beside_all = padded_2(field, (("lon", 1),), 1, True)
    return padded_2(beside_all, (("lat", 0),), 1, False)


def to_patches(tile):
    rows, cols, width = tile.shape
    shaped = tile.reshape(rows // PH, PH, cols // PW, PW, width)
    return shaped.transpose(0, 2, 1, 3, 4).reshape(-1, width)


def whole(shape):
    zeros = (0,) * len(shape)
    return pl.BlockSpec(shape, lambda *_: zeros)


def call(body, scalars, ins, outs, grid=(1,), in_specs=None, out_specs=None, scratch=(), alias=None):
    return pl.pallas_call(
        body,
        out_shape=outs,
        grid_spec=pltpu.PrefetchScalarGridSpec(
            num_scalar_prefetch=1,
            grid=grid,
            in_specs=in_specs or [whole(a.shape) for a in ins],
            out_specs=out_specs or [whole(o.shape) for o in outs],
            scratch_shapes=list(scratch),
        ),
        input_output_aliases=alias or {},
        compiler_params=pltpu.CompilerParams(vmem_limit_bytes=VMEM_LIMIT),
    )(scalars, *ins)


def shape_of(shape, dtype):
    return jax.ShapeDtypeStruct(shape, dtype)


def nt(left, right):
    return lax.dot_general(left, right, (((1,), (1,)), ((), ())), preferred_element_type=jnp.float32)


def lanes(at, size):
    return pl.ds(pl.multiple_of(at * size, size), size)


def pack(spectra_t, source, places, rows):
    channels = spectra_t.shape[0]

    def body(src, full, *refs):
        outs, sems = refs[:-1], refs[-1]
        copies = []
        for n, k in enumerate(places):
            for j in range(MOST):
                copies.append(
                    pltpu.make_async_copy(
                        full.at[:, lanes(src[k * MOST + j], rows)],
                        outs[n].at[:, j * rows : (j + 1) * rows],
                        sems.at[n * MOST + j],
                    )
                )
        for c in copies:
            c.start()
        for c in copies:
            c.wait()

    outs = [shape_of((channels, MOST * rows), spectra_t.dtype)] * len(places)
    return call(
        body,
        source,
        [spectra_t],
        outs,
        in_specs=[pl.BlockSpec(memory_space=pl.ANY)],
        scratch=[pltpu.SemaphoreType.DMA((len(places) * MOST,))],
    )


def spread_blocks(meta, first, arrived, weight_t, kernels, gain_col, before, patches, last):
    count = len(arrived)
    kernel_count, rows, cells = kernels.shape
    width = weight_t.shape[0]

    def body(meta_ref, *refs):
        xs = refs[:count]
        w, kern, g = refs[count : count + 3]
        spread, slope, *rest = refs[count + 3 + (before is not None) :]
        if before is None:
            spread[...] = jnp.zeros_like(spread)
        else:
            spread[...] = refs[count + 3][...]
        for k in range(count):
            pre = jnp.dot(w[...], xs[k][...], preferred_element_type=jnp.float32)
            s = jax.nn.sigmoid(pre)
            slope[k] = (s * (1.0 + pre * (1.0 - s))).astype(jnp.bfloat16)
            enc = (pre * s).astype(jnp.bfloat16)
            for j in range(MOST):
                code = meta_ref[(first + k) * MOST + j]

                @pl.when(code >= 0)
                def _():
                    spread[code // kernel_count] += jnp.dot(
                        enc[:, j * rows : (j + 1) * rows],
                        kern[code % kernel_count],
                        preferred_element_type=jnp.float32,
                    )

        if last:
            for q in range(patches):
                cell = spread[q]
                r = lax.rsqrt(jnp.mean(cell * cell, axis=0, keepdims=True) + EPS)
                rest[0][:, q * cells : (q + 1) * cells] = (cell * r * g[...]).astype(jnp.bfloat16)

    outs = [
        shape_of((patches, width, cells), jnp.float32),
        shape_of((count, width, MOST * rows), jnp.bfloat16),
    ]
    if last:
        outs.append(shape_of((width, patches * cells), jnp.bfloat16))
    ins = [*arrived, weight_t, kernels, gain_col] + ([] if before is None else [before])
    return call(body, meta, ins, outs)


def backward(meta, arrived, kernels_t, gain_col, spread, slopes, d_normed_t):
    count = len(arrived)
    groups = len(slopes)
    place_of = [(n, k) for n, one in enumerate(slopes) for k in range(one.shape[0])]
    kernel_count, cells, rows = kernels_t.shape
    patches, width, _ = spread.shape
    channels = arrived[0].shape[0]

    def body(meta_ref, *refs):
        xs = refs[:count]
        slos = refs[count : count + groups]
        kern, g, spr, dn, out, dsp, dpre = refs[count + groups :]
        total = jnp.zeros((width, 1), jnp.float32)
        for q in range(patches):
            cell = spr[q]
            d = dn[:, q * cells : (q + 1) * cells]
            r = lax.rsqrt(jnp.mean(cell * cell, axis=0, keepdims=True) + EPS)
            unit = cell * r
            total = total + jnp.sum(d * unit, axis=1, keepdims=True)
            dg = d * g[...]
            inner = jnp.mean(dg * unit, axis=0, keepdims=True)
            dsp[q] = ((dg - unit * inner) * r).astype(jnp.bfloat16)
        out[...] = jnp.zeros_like(out)
        out[:, channels : channels + 1] = total
        for k in range(count):
            for j in range(MOST):
                code = meta_ref[k * MOST + j]
                span = slice(j * rows, (j + 1) * rows)

                @pl.when(code >= 0)
                def _():
                    drow = jnp.dot(
                        dsp[code // kernel_count],
                        kern[code % kernel_count],
                        preferred_element_type=jnp.float32,
                    ).astype(jnp.bfloat16)
                    dpre[:, span] = (
                        drow.astype(jnp.float32) * slos[place_of[k][0]][place_of[k][1], :, span].astype(jnp.float32)
                    ).astype(jnp.bfloat16)

                @pl.when(code < 0)
                def _():
                    dpre[:, span] = jnp.zeros((width, rows), jnp.bfloat16)

            out[:, :channels] += nt(dpre[...], xs[k][...])

    ins = [*arrived, *slopes, kernels_t, gain_col, spread, d_normed_t]
    outs = [shape_of((width, (channels // LANES + 1) * LANES), jnp.float32)]
    scratch = [
        pltpu.VMEM((patches, width, cells), jnp.bfloat16),
        pltpu.VMEM((width, MOST * rows), jnp.bfloat16),
    ]
    return call(body, meta, ins, outs, scratch=scratch)[0]


def place(half, part, taps, lane, scale, into=None):
    rows = part.shape[0]
    steps = 8
    unit = rows // steps

    def body(half_ref, piece, *refs):
        for t in range(taps):
            refs[-1][t] = piece[:, t * lane : (t + 1) * lane].astype(jnp.float32) * scale

    specs = [pl.BlockSpec((unit, part.shape[1]), lambda i, h: (i, 0))]
    ins = [part]
    if into is not None:
        ins.append(into)
        specs.append(pl.BlockSpec(memory_space=pl.ANY))
    return call(
        body,
        half.reshape(1),
        ins,
        [shape_of((taps, 2 * rows, lane), jnp.float32)],
        grid=(steps,),
        in_specs=specs,
        out_specs=[pl.BlockSpec((taps, unit, lane), lambda i, h: (0, h[0] * steps + i, 0))],
        alias=None if into is None else {2: 0},
    )[0]


def shards(
    spectra,
    block_target,
    block_patch,
    block_kernel,
    encoder_weight,
    kernels,
    gain,
    conv_weight,
    cotangent,
):
    lons = lax.axis_size("lon")
    lats = lax.axis_size("lat")
    lon = lax.axis_index("lon")
    blocks = block_target.shape[0]
    kernel_count, block_rows, _ = kernels.shape
    channels = spectra.shape[1]
    width = encoder_weight.shape[1]
    tile_rows, tile_cols = (cotangent.shape[0], cotangent.shape[1])
    loss_scale = 1.0 / math.sqrt(tile_rows * lats * tile_cols * lons)
    cells = tile_rows * tile_cols

    cot_beside = padded_2(cotangent, (("lon", 1),), 1, True)
    order = lon ^ jnp.arange(lons, dtype=jnp.int32)
    hit = (block_target[:, None] == order[None, :]).astype(jnp.int32)
    rank = jnp.cumsum(hit, axis=0) - hit
    chosen = hit[:, :, None] * (rank[:, :, None] == jnp.arange(MOST)[None, None, :]).astype(jnp.int32)
    number = jnp.arange(blocks, dtype=jnp.int32)
    source = jnp.sum(chosen * number[:, None, None], axis=0).reshape(-1)
    code = block_patch * kernel_count + block_kernel + 1
    codes = jnp.sum(chosen * code[:, None, None], axis=0) - 1
    spectra_t = spectra.T
    far, near = range(lons // 2, lons), range(lons // 2)
    packed = dict(zip(far, pack(spectra_t, source, far, block_rows)))
    packed |= zip(near, pack(spectra_t, source, near, block_rows))
    cot_padded = padded_2(cot_beside, (("lat", 0),), 1, False)

    by_tile = jnp.sum(
        jnp.where((order[None, :] == jnp.arange(lons)[:, None])[:, :, None], codes[None], 0), axis=1
    )
    came = lax.all_to_all(by_tile, "lon", 0, 0, tiled=True)
    meta = jnp.sum(
        jnp.where((order[:, None] == jnp.arange(lons)[None, :])[:, :, None], came[None], 0), axis=1
    ).reshape(-1)

    arrived = [packed[0]] + [None] * (lons - 1)
    for k in [*far, *near[1:]]:
        arrived[k] = exchange(packed[k], lats, lons, lambda a, b, k=k: (a, b ^ k))

    windows = jnp.concatenate(
        [
            to_patches(cot_padded[2 - a : 2 - a + tile_rows, 2 - b : 2 - b + tile_cols])
            for a in range(3)
            for b in range(3)
        ],
        axis=1,
    )
    taps = 9
    weight_all = conv_weight.reshape(taps, width, width).transpose(1, 0, 2).reshape(width, -1)
    d_normed_t = nt(weight_all, windows)

    meta, d_normed_t, windows = lax.optimization_barrier((meta, d_normed_t, windows))
    patches = tile_rows // PH * (tile_cols // PW)
    gain_col = gain.reshape(width, 1)
    weight_t = encoder_weight.T
    cuts = [0, lons // 2, lons - 1, lons]
    spread, slopes = None, []
    for low, high in zip(cuts, cuts[1:]):
        last = high == lons
        spread, slope, *rest = spread_blocks(
            meta, low, arrived[low:high], weight_t, kernels, gain_col, spread, patches, last
        )
        slopes.append(slope)
    normed_t = rest[0]

    plan = stage_plan(lats, lons)
    lat = lax.axis_index("lat")
    halves = [kept_half(masks, lat, lon) for _, masks in plan]
    core = halves[0]
    away = jnp.dot(
        pick(normed_t, 1 - core), windows, preferred_element_type=jnp.float32
    ).astype(jnp.bfloat16)
    keep = jnp.dot(pick(normed_t, core), windows, preferred_element_type=jnp.float32)
    came = step(away, plan[0][0], lats, lons)

    small = backward(
        meta, arrived, kernels.transpose(0, 2, 1), gain_col, spread, slopes, d_normed_t
    )
    small_keep = pick(small, core)
    small_came = step(pick(small, 1 - core).astype(jnp.bfloat16), plan[0][0], lats, lons)

    apart = len(plan) - 2
    for n in range(1, apart):
        away, keep = split_sum(keep, came, halves[n])
        came = step(away, plan[n][0], lats, lons)
        away, small_keep = split_sum(small_keep, small_came, halves[n])
        small_came = step(away, plan[n][0], lats, lons)
    wide = taps * width
    keep = jnp.concatenate([keep, small_keep], axis=1)
    came = jnp.concatenate([came, small_came], axis=1)
    for n in range(apart, len(plan)):
        away, keep = split_sum(keep, came, halves[n])
        came = step(away, plan[n][0], lats, lons)
    normed = normed_t.reshape(width, tile_rows // PH, tile_cols // PW, PH, PW)
    normed = normed.transpose(1, 3, 2, 4, 0).reshape(tile_rows, tile_cols, width)
    padded = widen(normed)
    result_sum = jnp.zeros((cells, width), jnp.float32)
    for a in range(3):
        for b in range(3):
            window = padded[a : a + tile_rows, b : b + tile_cols].reshape(-1, width)
            result_sum = result_sum + jnp.dot(
                window, conv_weight[a, b], preferred_element_type=jnp.float32
            )
    conv_out = result_sum.reshape(tile_rows, tile_cols, width).astype(jnp.bfloat16)
    part = (keep + came.astype(jnp.float32)).astype(jnp.bfloat16)
    for n in range(len(plan) - 1, 0, -1):
        if n == 1:
            part, conv_out = lax.optimization_barrier((part, conv_out))
        other = step(part, plan[n][0], lats, lons)
        part = jnp.where(
            halves[n] == 0, jnp.concatenate([part, other]), jnp.concatenate([other, part])
        )
    others = step(part, plan[0][0], lats, lons)
    conv_total = place(core, part, taps, width, loss_scale)
    conv_total = place(1 - core, others, taps, width, loss_scale, conv_total)
    mine, theirs = part[:, wide:], others[:, wide:]
    small = jnp.where(
        core == 0, jnp.concatenate([mine, theirs]), jnp.concatenate([theirs, mine])
    ).astype(jnp.float32) * loss_scale
    gain_total = small[:, channels]
    encoder_total = small[:, :channels].T

    return (conv_out, conv_total.reshape(3, 3, width, width), encoder_total, gain_total)


def solution(mesh):
    placed = (
        P(("lat", "lon"), None),
        P(("lat", "lon")),
        P(("lat", "lon")),
        P(("lat", "lon")),
        P(),
        P(),
        P(),
        P(),
        P("lat", "lon", None),
    )

    return jax.shard_map(
        shards,
        mesh=mesh,
        in_specs=placed,
        out_specs=(P("lat", "lon", None), P(), P(), P()),
        check_vma=False,
    )
```

```python
import math

import jax
import jax.numpy as jnp
from jax import lax
from jax.experimental import pallas as pl
from jax.experimental.pallas import tpu as pltpu
from jax.sharding import PartitionSpec as P


PH = 8
PW = 16
MOST = 3
EPS = 1e-06
LANES = 128
AXES = ("lat", "lon")
VMEM_LIMIT = 24 * 1024 * 1024


def bits_of(count):
    assert count & (count - 1) == 0
    return [1 << i for i in range(count.bit_length() - 1)]


def parity(value, mask):
    out = jnp.zeros((), jnp.int32)
    while mask:
        low = mask & -mask
        out = out ^ ((value & low) != 0).astype(jnp.int32)
        mask ^= low
    return out


def exchange(value, lats, lons, move):
    pairs = []
    for a in range(lats):
        for b in range(lons):
            c, d = move(a, b)
            pairs.append((a * lons + b, c * lons + d))
    return lax.ppermute(value, AXES, pairs)


def stage_plan(lats, lons):
    lat_bits, lon_bits = bits_of(lats), bits_of(lons)
    first = lat_bits[:1]
    lat_rest = lat_bits[1:]
    low, high = lon_bits[:1], lon_bits[1:]
    plan = [(((m, 0), (m, 0)), ((m, 0), (m, 0))) for m in first]
    ab = [(m, 0) for m in lat_rest] + [(0, m) for m in low]
    ba = [(0, m) for m in low] + [(m, 0) for m in lat_rest]
    plan += [((p, q), (p, q)) for p, q in zip(ab, ba)]
    if len(high) == 2:
        one, two = high
        plan += [(((0, one),) * 2, ((0, one | two),) * 2), (((0, one | two),) * 2, ((0, two),) * 2)]
    else:
        plan += [(((0, m),) * 2, ((0, m),) * 2) for m in high]
    return plan


def kept_half(masks, lat, lon):
    even = parity(lat, masks[0][0]) ^ parity(lon, masks[0][1])
    odd = parity(lat, masks[1][0]) ^ parity(lon, masks[1][1])
    return jnp.where((lat & 1) == 0, even, odd)


def step(value, steps, lats, lons):
    return exchange(value, lats, lons, lambda a, b: (a ^ steps[a & 1][0], b ^ steps[a & 1][1]))


def pick(value, half):
    pair = value.reshape(2, value.shape[0] // 2, value.shape[1])
    return lax.dynamic_index_in_dim(pair, half, 0, keepdims=False)


def split_sum(keep, came, half):
    away = pick(keep, 1 - half) + pick(came, 1 - half).astype(jnp.float32)
    stay = pick(keep, half) + pick(came, half).astype(jnp.float32)
    return away.astype(jnp.bfloat16), stay


def padded_2(shard, sides, width, wrap):
    for axis, dim in sides:
        size, length = (lax.axis_size(axis), shard.shape[dim])
        up = [(i, (i + 1) % size) for i in range(size if wrap else size - 1)]
        down = [(j, i) for i, j in up]
        last = lax.slice_in_dim(shard, length - width, length, axis=dim)
        leading = lax.slice_in_dim(shard, 0, width, axis=dim)
        before = lax.ppermute(last, axis, up)
        after = lax.ppermute(leading, axis, down)
        shard = jnp.concatenate([before, shard, after], axis=dim)
    return shard


def widen(field):
    beside_all = padded_2(field, (("lon", 1),), 1, True)
    return padded_2(beside_all, (("lat", 0),), 1, False)


def to_patches(tile):
    rows, cols, width = tile.shape
    shaped = tile.reshape(rows // PH, PH, cols // PW, PW, width)
    return shaped.transpose(0, 2, 1, 3, 4).reshape(-1, width)


def whole(shape):
    zeros = (0,) * len(shape)
    return pl.BlockSpec(shape, lambda *_: zeros, pipeline_mode=pl.Buffered(1))


def call(body, scalars, ins, outs, grid=(1,), in_specs=None, out_specs=None, scratch=(), alias=None):
    return pl.pallas_call(
        body,
        out_shape=outs,
        grid_spec=pltpu.PrefetchScalarGridSpec(
            num_scalar_prefetch=1,
            grid=grid,
            in_specs=in_specs or [whole(a.shape) for a in ins],
            out_specs=out_specs or [whole(o.shape) for o in outs],
            scratch_shapes=list(scratch),
        ),
        input_output_aliases=alias or {},
        compiler_params=pltpu.CompilerParams(vmem_limit_bytes=VMEM_LIMIT),
    )(scalars, *ins)


def shape_of(shape, dtype):
    return jax.ShapeDtypeStruct(shape, dtype)


def nt(left, right):
    return lax.dot_general(left, right, (((1,), (1,)), ((), ())), preferred_element_type=jnp.float32)


def lanes(at, size):
    return pl.ds(pl.multiple_of(at * size, size), size)


def pack(spectra_t, source, places, rows):
    channels = spectra_t.shape[0]

    def body(src, full, *refs):
        outs, sems = refs[:-1], refs[-1]
        copies = []
        for n, k in enumerate(places):
            for j in range(MOST):
                copies.append(
                    pltpu.make_async_copy(
                        full.at[:, lanes(src[k * MOST + j], rows)],
                        outs[n].at[:, j * rows : (j + 1) * rows],
                        sems.at[n * MOST + j],
                    )
                )
        for c in copies:
            c.start()
        for c in copies:
            c.wait()

    outs = [shape_of((channels, MOST * rows), spectra_t.dtype)] * len(places)
    return call(
        body,
        source,
        [spectra_t],
        outs,
        in_specs=[pl.BlockSpec(memory_space=pl.ANY)],
        scratch=[pltpu.SemaphoreType.DMA((len(places) * MOST,))],
    )


def spread_blocks(meta, first, arrived, weight_t, kernels, gain_col, before, patches, last):
    count = len(arrived)
    kernel_count, rows, cells = kernels.shape
    width = weight_t.shape[0]

    def body(meta_ref, *refs):
        xs = refs[:count]
        w, kern, g = refs[count : count + 3]
        spread, slope, *rest = refs[count + 3 + (before is not None) :]
        if before is None:
            spread[...] = jnp.zeros_like(spread)
        else:
            spread[...] = refs[count + 3][...]
        for k in range(count):
            pre = jnp.dot(w[...], xs[k][...], preferred_element_type=jnp.float32)
            s = jax.nn.sigmoid(pre)
            slope[k] = (s * (1.0 + pre * (1.0 - s))).astype(jnp.bfloat16)
            enc = (pre * s).astype(jnp.bfloat16)
            for j in range(MOST):
                code = meta_ref[(first + k) * MOST + j]

                @pl.when(code >= 0)
                def _():
                    spread[code // kernel_count] += jnp.dot(
                        enc[:, j * rows : (j + 1) * rows],
                        kern[code % kernel_count],
                        preferred_element_type=jnp.float32,
                    )

        if last:
            for q in range(patches):
                cell = spread[q]
                r = lax.rsqrt(jnp.mean(cell * cell, axis=0, keepdims=True) + EPS)
                rest[0][:, q * cells : (q + 1) * cells] = (cell * r * g[...]).astype(jnp.bfloat16)

    outs = [
        shape_of((patches, width, cells), jnp.float32),
        shape_of((count, width, MOST * rows), jnp.bfloat16),
    ]
    if last:
        outs.append(shape_of((width, patches * cells), jnp.bfloat16))
    ins = [*arrived, weight_t, kernels, gain_col] + ([] if before is None else [before])
    return call(body, meta, ins, outs)


def backward(meta, arrived, kernels_t, gain_col, spread, slopes, d_normed_t):
    count = len(arrived)
    groups = len(slopes)
    place_of = [(n, k) for n, one in enumerate(slopes) for k in range(one.shape[0])]
    kernel_count, cells, rows = kernels_t.shape
    patches, width, _ = spread.shape
    channels = arrived[0].shape[0]

    def body(meta_ref, *refs):
        xs = refs[:count]
        slos = refs[count : count + groups]
        kern, g, spr, dn, out, dsp, dpre = refs[count + groups :]
        total = jnp.zeros((width, 1), jnp.float32)
        for q in range(patches):
            cell = spr[q]
            d = dn[:, q * cells : (q + 1) * cells]
            r = lax.rsqrt(jnp.mean(cell * cell, axis=0, keepdims=True) + EPS)
            unit = cell * r
            total = total + jnp.sum(d * unit, axis=1, keepdims=True)
            dg = d * g[...]
            inner = jnp.mean(dg * unit, axis=0, keepdims=True)
            dsp[q] = ((dg - unit * inner) * r).astype(jnp.bfloat16)
        out[...] = jnp.zeros_like(out)
        out[:, channels : channels + 1] = total
        for k in range(count):
            for j in range(MOST):
                code = meta_ref[k * MOST + j]
                span = slice(j * rows, (j + 1) * rows)

                @pl.when(code >= 0)
                def _():
                    drow = jnp.dot(
                        dsp[code // kernel_count],
                        kern[code % kernel_count],
                        preferred_element_type=jnp.float32,
                    ).astype(jnp.bfloat16)
                    dpre[:, span] = (
                        drow.astype(jnp.float32) * slos[place_of[k][0]][place_of[k][1], :, span].astype(jnp.float32)
                    ).astype(jnp.bfloat16)

                @pl.when(code < 0)
                def _():
                    dpre[:, span] = jnp.zeros((width, rows), jnp.bfloat16)

            out[:, :channels] += nt(dpre[...], xs[k][...])

    ins = [*arrived, *slopes, kernels_t, gain_col, spread, d_normed_t]
    outs = [shape_of((width, (channels // LANES + 1) * LANES), jnp.float32)]
    scratch = [
        pltpu.VMEM((patches, width, cells), jnp.bfloat16),
        pltpu.VMEM((width, MOST * rows), jnp.bfloat16),
    ]
    return call(body, meta, ins, outs, scratch=scratch)[0]


def place(quarter, part, taps, lane, channels, scale, into=None):
    rows = part.shape[0]
    steps = 2
    unit = rows // steps

    def body(at, piece, small, *refs):
        conv, encoder, gain = refs[-3:]
        for t in range(taps):
            conv[t] = piece[:, t * lane : (t + 1) * lane].astype(jnp.float32) * scale

        @pl.when(pl.program_id(0) == 0)
        def _():
            turned = (small[...].astype(jnp.float32) * scale).T
            encoder[...] = turned[:channels]
            gain[...] = turned[channels : channels + 1]

    wide = taps * lane
    extra = part.shape[1] - wide
    specs = [
        pl.BlockSpec((unit, wide), lambda i, q: (i, 0)),
        pl.BlockSpec((rows, extra), lambda i, q: (0, 0)),
    ]
    ins = [part, part[:, wide:]]
    if into is not None:
        ins += list(into)
        specs += [pl.BlockSpec(memory_space=pl.ANY)] * 3
    return call(
        body,
        quarter.reshape(1),
        ins,
        [
            shape_of((taps, 4 * rows, lane), jnp.float32),
            shape_of((channels, 4 * rows), jnp.float32),
            shape_of((1, 4 * rows), jnp.float32),
        ],
        grid=(steps,),
        in_specs=specs,
        out_specs=[
            pl.BlockSpec((taps, unit, lane), lambda i, q: (0, q[0] * steps + i, 0)),
            pl.BlockSpec((channels, rows), lambda i, q: (0, q[0])),
            pl.BlockSpec((1, rows), lambda i, q: (0, q[0])),
        ],
        alias=None if into is None else {3: 0, 4: 1, 5: 2},
    )


def shards(
    spectra,
    block_target,
    block_patch,
    block_kernel,
    encoder_weight,
    kernels,
    gain,
    conv_weight,
    cotangent,
):
    lons = lax.axis_size("lon")
    lats = lax.axis_size("lat")
    lon = lax.axis_index("lon")
    blocks = block_target.shape[0]
    kernel_count, block_rows, _ = kernels.shape
    channels = spectra.shape[1]
    width = encoder_weight.shape[1]
    tile_rows, tile_cols = (cotangent.shape[0], cotangent.shape[1])
    loss_scale = 1.0 / math.sqrt(tile_rows * lats * tile_cols * lons)
    cells = tile_rows * tile_cols

    cot_beside = padded_2(cotangent, (("lon", 1),), 1, True)
    order = lon ^ jnp.arange(lons, dtype=jnp.int32)
    hit = (block_target[:, None] == order[None, :]).astype(jnp.int32)
    rank = jnp.cumsum(hit, axis=0) - hit
    chosen = hit[:, :, None] * (rank[:, :, None] == jnp.arange(MOST)[None, None, :]).astype(jnp.int32)
    number = jnp.arange(blocks, dtype=jnp.int32)
    source = jnp.sum(chosen * number[:, None, None], axis=0).reshape(-1)
    code = block_patch * kernel_count + block_kernel + 1
    codes = jnp.sum(chosen * code[:, None, None], axis=0) - 1
    spectra_t = spectra.T
    far, near = range(lons // 2, lons), range(lons // 2)
    packed = dict(zip(far, pack(spectra_t, source, far, block_rows)))
    packed |= zip(near, pack(spectra_t, source, near, block_rows))
    cot_padded = padded_2(cot_beside, (("lat", 0),), 1, False)

    by_tile = jnp.sum(
        jnp.where((order[None, :] == jnp.arange(lons)[:, None])[:, :, None], codes[None], 0), axis=1
    )
    came = lax.all_to_all(by_tile, "lon", 0, 0, tiled=True)
    meta = jnp.sum(
        jnp.where((order[:, None] == jnp.arange(lons)[None, :])[:, :, None], came[None], 0), axis=1
    ).reshape(-1)

    arrived = [packed[0]] + [None] * (lons - 1)
    for k in [*far, *near[1:]]:
        arrived[k] = exchange(packed[k], lats, lons, lambda a, b, k=k: (a, b ^ k))

    windows = jnp.concatenate(
        [
            to_patches(cot_padded[2 - a : 2 - a + tile_rows, 2 - b : 2 - b + tile_cols])
            for a in range(3)
            for b in range(3)
        ],
        axis=1,
    )
    taps = 9
    weight_all = conv_weight.reshape(taps, width, width).transpose(1, 0, 2).reshape(width, -1)
    d_normed_t = nt(weight_all, windows)

    meta, d_normed_t, windows = lax.optimization_barrier((meta, d_normed_t, windows))
    patches = tile_rows // PH * (tile_cols // PW)
    gain_col = gain.reshape(width, 1)
    weight_t = encoder_weight.T
    cuts = [0, lons // 2, lons - 1, lons]
    spread, slopes = None, []
    for low, high in zip(cuts, cuts[1:]):
        last = high == lons
        spread, slope, *rest = spread_blocks(
            meta, low, arrived[low:high], weight_t, kernels, gain_col, spread, patches, last
        )
        slopes.append(slope)
    normed_t = rest[0]

    plan = stage_plan(lats, lons)
    lat = lax.axis_index("lat")
    halves = [kept_half(masks, lat, lon) for _, masks in plan]
    core = halves[0]
    away = jnp.dot(
        pick(normed_t, 1 - core), windows, preferred_element_type=jnp.float32
    ).astype(jnp.bfloat16)
    keep = jnp.dot(pick(normed_t, core), windows, preferred_element_type=jnp.float32)
    came = step(away, plan[0][0], lats, lons)

    away, keep = split_sum(keep, came, halves[1])
    away, spread = lax.optimization_barrier((away, spread))
    came = step(away, plan[1][0], lats, lons)
    small = backward(
        meta, arrived, kernels.transpose(0, 2, 1), gain_col, spread, slopes, d_normed_t
    )
    small_keep = pick(small, core)
    small_came = step(pick(small, 1 - core).astype(jnp.bfloat16), plan[0][0], lats, lons)

    away, small_keep = split_sum(small_keep, small_came, halves[1])
    small_came = step(away, plan[1][0], lats, lons)
    apart = len(plan) - 2
    for n in range(2, apart):
        away, keep = split_sum(keep, came, halves[n])
        came = step(away, plan[n][0], lats, lons)
        away, small_keep = split_sum(small_keep, small_came, halves[n])
        small_came = step(away, plan[n][0], lats, lons)
    keep = jnp.concatenate([keep, small_keep], axis=1)
    came = jnp.concatenate([came, small_came], axis=1)
    for n in range(apart, len(plan)):
        away, keep = split_sum(keep, came, halves[n])
        came = step(away, plan[n][0], lats, lons)
    normed = normed_t.reshape(width, tile_rows // PH, tile_cols // PW, PH, PW)
    normed = normed.transpose(1, 3, 2, 4, 0).reshape(tile_rows, tile_cols, width)
    padded = widen(normed)
    result_sum = jnp.zeros((cells, width), jnp.float32)
    for a in range(3):
        for b in range(3):
            window = padded[a : a + tile_rows, b : b + tile_cols].reshape(-1, width)
            result_sum = result_sum + jnp.dot(
                window, conv_weight[a, b], preferred_element_type=jnp.float32
            )
    conv_out = result_sum.reshape(tile_rows, tile_cols, width).astype(jnp.bfloat16)
    part = (keep + came.astype(jnp.float32)).astype(jnp.bfloat16)
    for n in range(len(plan) - 1, 1, -1):
        other = step(part, plan[n][0], lats, lons)
        part = jnp.where(
            halves[n] == 0, jnp.concatenate([part, other]), jnp.concatenate([other, part])
        )
    part, conv_out = lax.optimization_barrier((part, conv_out))
    own, beside = halves[1], kept_half(plan[1][1], lat ^ 1, lon)
    other = step(part, plan[1][0], lats, lons)
    beside_part = step(part, plan[0][0], lats, lons)
    beside_other = step(other, plan[0][0], lats, lons)
    totals = None
    for quarter, value in (
        (2 * core + own, part),
        (2 * (1 - core) + beside, beside_part),
        (2 * core + 1 - own, other),
        (2 * (1 - core) + 1 - beside, beside_other),
    ):
        totals = place(quarter, value, taps, width, channels, loss_scale, totals)
    conv_total, encoder_total, gain_total = totals
    gain_total = gain_total[0]
    return (conv_out, conv_total.reshape(3, 3, width, width), encoder_total, gain_total)


def solution(mesh):
    placed = (
        P(("lat", "lon"), None),
        P(("lat", "lon")),
        P(("lat", "lon")),
        P(("lat", "lon")),
        P(),
        P(),
        P(),
        P(),
        P("lat", "lon", None),
    )

    return jax.shard_map(
        shards,
        mesh=mesh,
        in_specs=placed,
        out_specs=(P("lat", "lon", None), P(), P(), P()),
        check_vma=False,
    )
```

```python
import math

import jax
import jax.numpy as jnp
from jax import lax
from jax.experimental import pallas as pl
from jax.experimental.pallas import tpu as pltpu
from jax.sharding import PartitionSpec as P


PH = 8
PW = 16
MOST = 3
EPS = 1e-06
LANES = 128
AXES = ("lat", "lon")
VMEM_LIMIT = 24 * 1024 * 1024


def bits_of(count):
    assert count & (count - 1) == 0
    return [1 << i for i in range(count.bit_length() - 1)]


def parity(value, mask):
    out = jnp.zeros((), jnp.int32)
    while mask:
        low = mask & -mask
        out = out ^ ((value & low) != 0).astype(jnp.int32)
        mask ^= low
    return out


def exchange(value, lats, lons, move):
    pairs = []
    for a in range(lats):
        for b in range(lons):
            c, d = move(a, b)
            pairs.append((a * lons + b, c * lons + d))
    return lax.ppermute(value, AXES, pairs)


def stage_plan(lats, lons):
    lat_bits, lon_bits = bits_of(lats), bits_of(lons)
    first = lat_bits[:1]
    lat_rest = lat_bits[1:]
    low, high = lon_bits[:1], lon_bits[1:]
    plan = [(((m, 0), (m, 0)), ((m, 0), (m, 0))) for m in first]
    ab = [(m, 0) for m in lat_rest] + [(0, m) for m in low]
    ba = [(0, m) for m in low] + [(m, 0) for m in lat_rest]
    plan += [((p, q), (p, q)) for p, q in zip(ab, ba)]
    if len(high) == 2:
        one, two = high
        plan += [(((0, one),) * 2, ((0, one | two),) * 2), (((0, one | two),) * 2, ((0, two),) * 2)]
    else:
        plan += [(((0, m),) * 2, ((0, m),) * 2) for m in high]
    return plan


def kept_half(masks, lat, lon):
    even = parity(lat, masks[0][0]) ^ parity(lon, masks[0][1])
    odd = parity(lat, masks[1][0]) ^ parity(lon, masks[1][1])
    return jnp.where((lat & 1) == 0, even, odd)


def step(value, steps, lats, lons):
    return exchange(value, lats, lons, lambda a, b: (a ^ steps[a & 1][0], b ^ steps[a & 1][1]))


def pick(value, half):
    pair = value.reshape(2, value.shape[0] // 2, value.shape[1])
    return lax.dynamic_index_in_dim(pair, half, 0, keepdims=False)


def split_sum(keep, came, half):
    away = pick(keep, 1 - half) + pick(came, 1 - half).astype(jnp.float32)
    stay = pick(keep, half) + pick(came, half).astype(jnp.float32)
    return away.astype(jnp.bfloat16), stay


def padded_2(shard, sides, width, wrap):
    for axis, dim in sides:
        size, length = (lax.axis_size(axis), shard.shape[dim])
        up = [(i, (i + 1) % size) for i in range(size if wrap else size - 1)]
        down = [(j, i) for i, j in up]
        last = lax.slice_in_dim(shard, length - width, length, axis=dim)
        leading = lax.slice_in_dim(shard, 0, width, axis=dim)
        before = lax.ppermute(last, axis, up)
        after = lax.ppermute(leading, axis, down)
        shard = jnp.concatenate([before, shard, after], axis=dim)
    return shard


def widen(field):
    beside_all = padded_2(field, (("lon", 1),), 1, True)
    return padded_2(beside_all, (("lat", 0),), 1, False)


def to_patches(tile):
    rows, cols, width = tile.shape
    shaped = tile.reshape(rows // PH, PH, cols // PW, PW, width)
    return shaped.transpose(0, 2, 1, 3, 4).reshape(-1, width)


def whole(shape):
    zeros = (0,) * len(shape)
    return pl.BlockSpec(shape, lambda *_: zeros, pipeline_mode=pl.Buffered(1))


def call(body, scalars, ins, outs, grid=(1,), in_specs=None, out_specs=None, scratch=(), alias=None):
    return pl.pallas_call(
        body,
        out_shape=outs,
        grid_spec=pltpu.PrefetchScalarGridSpec(
            num_scalar_prefetch=1,
            grid=grid,
            in_specs=in_specs or [whole(a.shape) for a in ins],
            out_specs=out_specs or [whole(o.shape) for o in outs],
            scratch_shapes=list(scratch),
        ),
        input_output_aliases=alias or {},
        compiler_params=pltpu.CompilerParams(vmem_limit_bytes=VMEM_LIMIT),
    )(scalars, *ins)


def shape_of(shape, dtype):
    return jax.ShapeDtypeStruct(shape, dtype)


def nt(left, right):
    return lax.dot_general(left, right, (((1,), (1,)), ((), ())), preferred_element_type=jnp.float32)


def lanes(at, size):
    return pl.ds(pl.multiple_of(at * size, size), size)


def pack(spectra_t, source, places, rows):
    channels = spectra_t.shape[0]

    def body(src, full, *refs):
        outs, sems = refs[:-1], refs[-1]
        copies = []
        for n, k in enumerate(places):
            for j in range(MOST):
                copies.append(
                    pltpu.make_async_copy(
                        full.at[:, lanes(src[k * MOST + j], rows)],
                        outs[n].at[:, j * rows : (j + 1) * rows],
                        sems.at[n * MOST + j],
                    )
                )
        for c in copies:
            c.start()
        for c in copies:
            c.wait()

    outs = [shape_of((channels, MOST * rows), spectra_t.dtype)] * len(places)
    return call(
        body,
        source,
        [spectra_t],
        outs,
        in_specs=[pl.BlockSpec(memory_space=pl.ANY)],
        scratch=[pltpu.SemaphoreType.DMA((len(places) * MOST,))],
    )


def spread_blocks(meta, first, arrived, weight_t, kernels, gain_col, before, patches, last):
    count = len(arrived)
    kernel_count, rows, cells = kernels.shape
    width = weight_t.shape[0]

    def body(meta_ref, *refs):
        xs = refs[:count]
        w, kern, g = refs[count : count + 3]
        spread, slope, *rest = refs[count + 3 + (before is not None) :]
        if before is None:
            spread[...] = jnp.zeros_like(spread)
        else:
            spread[...] = refs[count + 3][...]
        for k in range(count):
            pre = jnp.dot(w[...], xs[k][...], preferred_element_type=jnp.float32)
            s = jax.nn.sigmoid(pre)
            slope[k] = (s * (1.0 + pre * (1.0 - s))).astype(jnp.bfloat16)
            enc = (pre * s).astype(jnp.bfloat16)
            for j in range(MOST):
                code = meta_ref[(first + k) * MOST + j]

                @pl.when(code >= 0)
                def _():
                    spread[code // kernel_count] += jnp.dot(
                        enc[:, j * rows : (j + 1) * rows],
                        kern[code % kernel_count],
                        preferred_element_type=jnp.float32,
                    )

        if last:
            for q in range(patches):
                cell = spread[q]
                r = lax.rsqrt(jnp.mean(cell * cell, axis=0, keepdims=True) + EPS)
                rest[0][:, q * cells : (q + 1) * cells] = (cell * r * g[...]).astype(jnp.bfloat16)

    outs = [
        shape_of((patches, width, cells), jnp.float32),
        shape_of((count, width, MOST * rows), jnp.bfloat16),
    ]
    if last:
        outs.append(shape_of((width, patches * cells), jnp.bfloat16))
    ins = [*arrived, weight_t, kernels, gain_col] + ([] if before is None else [before])
    return call(body, meta, ins, outs)


def backward(meta, arrived, kernels_t, gain_col, spread, slopes, d_normed_t):
    count = len(arrived)
    groups = len(slopes)
    place_of = [(n, k) for n, one in enumerate(slopes) for k in range(one.shape[0])]
    kernel_count, cells, rows = kernels_t.shape
    patches, width, _ = spread.shape
    channels = arrived[0].shape[0]

    def body(meta_ref, *refs):
        xs = refs[:count]
        slos = refs[count : count + groups]
        kern, g, spr, dn, out, dsp, dpre = refs[count + groups :]
        total = jnp.zeros((width, 1), jnp.float32)
        for q in range(patches):
            cell = spr[q]
            d = dn[:, q * cells : (q + 1) * cells]
            r = lax.rsqrt(jnp.mean(cell * cell, axis=0, keepdims=True) + EPS)
            unit = cell * r
            total = total + jnp.sum(d * unit, axis=1, keepdims=True)
            dg = d * g[...]
            inner = jnp.mean(dg * unit, axis=0, keepdims=True)
            dsp[q] = ((dg - unit * inner) * r).astype(jnp.bfloat16)
        out[...] = jnp.zeros_like(out)
        out[:, channels : channels + 1] = total
        for k in range(count):
            for j in range(MOST):
                code = meta_ref[k * MOST + j]
                span = slice(j * rows, (j + 1) * rows)

                @pl.when(code >= 0)
                def _():
                    drow = jnp.dot(
                        dsp[code // kernel_count],
                        kern[code % kernel_count],
                        preferred_element_type=jnp.float32,
                    ).astype(jnp.bfloat16)
                    dpre[:, span] = (
                        drow.astype(jnp.float32) * slos[place_of[k][0]][place_of[k][1], :, span].astype(jnp.float32)
                    ).astype(jnp.bfloat16)

                @pl.when(code < 0)
                def _():
                    dpre[:, span] = jnp.zeros((width, rows), jnp.bfloat16)

            out[:, :channels] += nt(dpre[...], xs[k][...])

    ins = [*arrived, *slopes, kernels_t, gain_col, spread, d_normed_t]
    outs = [shape_of((width, (channels // LANES + 1) * LANES), jnp.float32)]
    scratch = [
        pltpu.VMEM((patches, width, cells), jnp.bfloat16),
        pltpu.VMEM((width, MOST * rows), jnp.bfloat16),
    ]
    return call(body, meta, ins, outs, scratch=scratch)[0]


def place(quarter, part, taps, lane, channels, scale, into=None):
    rows = part.shape[0]
    steps = 2
    unit = rows // steps

    def body(at, piece, small, *refs):
        conv, encoder, gain = refs[-3:]
        for t in range(taps):
            conv[t] = piece[:, t * lane : (t + 1) * lane].astype(jnp.float32) * scale

        @pl.when(pl.program_id(0) == 0)
        def _():
            turned = (small[:, taps * lane :].astype(jnp.float32) * scale).T
            encoder[...] = turned[:channels]
            gain[...] = turned[channels : channels + 1]

    specs = [pl.BlockSpec((unit, part.shape[1]), lambda i, q: (i, 0)), whole(part.shape)]
    ins = [part, part]
    if into is not None:
        ins += list(into)
        specs += [pl.BlockSpec(memory_space=pl.ANY)] * 3
    return call(
        body,
        quarter.reshape(1),
        ins,
        [
            shape_of((taps, 4 * rows, lane), jnp.float32),
            shape_of((channels, 4 * rows), jnp.float32),
            shape_of((1, 4 * rows), jnp.float32),
        ],
        grid=(steps,),
        in_specs=specs,
        out_specs=[
            pl.BlockSpec((taps, unit, lane), lambda i, q: (0, q[0] * steps + i, 0)),
            pl.BlockSpec((channels, rows), lambda i, q: (0, q[0])),
            pl.BlockSpec((1, rows), lambda i, q: (0, q[0])),
        ],
        alias=None if into is None else {3: 0, 4: 1, 5: 2},
    )


def shards(
    spectra,
    block_target,
    block_patch,
    block_kernel,
    encoder_weight,
    kernels,
    gain,
    conv_weight,
    cotangent,
):
    lons = lax.axis_size("lon")
    lats = lax.axis_size("lat")
    lon = lax.axis_index("lon")
    blocks = block_target.shape[0]
    kernel_count, block_rows, _ = kernels.shape
    channels = spectra.shape[1]
    width = encoder_weight.shape[1]
    tile_rows, tile_cols = (cotangent.shape[0], cotangent.shape[1])
    loss_scale = 1.0 / math.sqrt(tile_rows * lats * tile_cols * lons)
    cells = tile_rows * tile_cols

    cot_beside = padded_2(cotangent, (("lon", 1),), 1, True)
    order = lon ^ jnp.arange(lons, dtype=jnp.int32)
    hit = (block_target[:, None] == order[None, :]).astype(jnp.int32)
    rank = jnp.cumsum(hit, axis=0) - hit
    chosen = hit[:, :, None] * (rank[:, :, None] == jnp.arange(MOST)[None, None, :]).astype(jnp.int32)
    number = jnp.arange(blocks, dtype=jnp.int32)
    source = jnp.sum(chosen * number[:, None, None], axis=0).reshape(-1)
    code = block_patch * kernel_count + block_kernel + 1
    codes = jnp.sum(chosen * code[:, None, None], axis=0) - 1
    spectra_t = spectra.T
    far, near = range(lons // 2, lons), range(lons // 2)
    packed = dict(zip(far, pack(spectra_t, source, far, block_rows)))
    packed |= zip(near, pack(spectra_t, source, near, block_rows))
    cot_padded = padded_2(cot_beside, (("lat", 0),), 1, False)

    by_tile = jnp.sum(
        jnp.where((order[None, :] == jnp.arange(lons)[:, None])[:, :, None], codes[None], 0), axis=1
    )
    came = lax.all_to_all(by_tile, "lon", 0, 0, tiled=True)
    meta = jnp.sum(
        jnp.where((order[:, None] == jnp.arange(lons)[None, :])[:, :, None], came[None], 0), axis=1
    ).reshape(-1)

    arrived = [packed[0]] + [None] * (lons - 1)
    for k in [*far, *near[1:]]:
        arrived[k] = exchange(packed[k], lats, lons, lambda a, b, k=k: (a, b ^ k))

    windows = jnp.concatenate(
        [
            to_patches(cot_padded[2 - a : 2 - a + tile_rows, 2 - b : 2 - b + tile_cols])
            for a in range(3)
            for b in range(3)
        ],
        axis=1,
    )
    taps = 9
    weight_all = conv_weight.reshape(taps, width, width).transpose(1, 0, 2).reshape(width, -1)
    d_normed_t = nt(weight_all, windows)

    meta, d_normed_t, windows = lax.optimization_barrier((meta, d_normed_t, windows))
    patches = tile_rows // PH * (tile_cols // PW)
    gain_col = gain.reshape(width, 1)
    weight_t = encoder_weight.T
    cuts = [0, lons // 2, lons - 1, lons]
    spread, slopes = None, []
    for low, high in zip(cuts, cuts[1:]):
        last = high == lons
        spread, slope, *rest = spread_blocks(
            meta, low, arrived[low:high], weight_t, kernels, gain_col, spread, patches, last
        )
        slopes.append(slope)
    normed_t = rest[0]

    plan = stage_plan(lats, lons)
    lat = lax.axis_index("lat")
    halves = [kept_half(masks, lat, lon) for _, masks in plan]
    core = halves[0]
    away = jnp.dot(
        pick(normed_t, 1 - core), windows, preferred_element_type=jnp.float32
    ).astype(jnp.bfloat16)
    keep = jnp.dot(pick(normed_t, core), windows, preferred_element_type=jnp.float32)
    came = step(away, plan[0][0], lats, lons)

    away, keep = split_sum(keep, came, halves[1])
    away, spread = lax.optimization_barrier((away, spread))
    came = step(away, plan[1][0], lats, lons)
    small = backward(
        meta, arrived, kernels.transpose(0, 2, 1), gain_col, spread, slopes, d_normed_t
    )
    small_keep = pick(small, core)
    small_came = step(pick(small, 1 - core).astype(jnp.bfloat16), plan[0][0], lats, lons)

    away, small_keep = split_sum(small_keep, small_came, halves[1])
    small_came = step(away, plan[1][0], lats, lons)
    apart = len(plan) - 2
    for n in range(2, apart):
        away, keep = split_sum(keep, came, halves[n])
        came = step(away, plan[n][0], lats, lons)
        away, small_keep = split_sum(small_keep, small_came, halves[n])
        small_came = step(away, plan[n][0], lats, lons)
    keep = jnp.concatenate([keep, small_keep], axis=1)
    came = jnp.concatenate([came, small_came], axis=1)
    for n in range(apart, len(plan)):
        away, keep = split_sum(keep, came, halves[n])
        came = step(away, plan[n][0], lats, lons)
    normed = normed_t.reshape(width, tile_rows // PH, tile_cols // PW, PH, PW)
    normed = normed.transpose(1, 3, 2, 4, 0).reshape(tile_rows, tile_cols, width)
    padded = widen(normed)
    result_sum = jnp.zeros((cells, width), jnp.float32)
    for a in range(3):
        for b in range(3):
            window = padded[a : a + tile_rows, b : b + tile_cols].reshape(-1, width)
            result_sum = result_sum + jnp.dot(
                window, conv_weight[a, b], preferred_element_type=jnp.float32
            )
    conv_out = result_sum.reshape(tile_rows, tile_cols, width).astype(jnp.bfloat16)
    part = (keep + came.astype(jnp.float32)).astype(jnp.bfloat16)
    for n in range(len(plan) - 1, 1, -1):
        other = step(part, plan[n][0], lats, lons)
        part = jnp.where(
            halves[n] == 0, jnp.concatenate([part, other]), jnp.concatenate([other, part])
        )
    part, conv_out = lax.optimization_barrier((part, conv_out))
    own, beside = halves[1], kept_half(plan[1][1], lat ^ 1, lon)
    other = step(part, plan[1][0], lats, lons)
    beside_part = step(part, plan[0][0], lats, lons)
    beside_other = step(other, plan[0][0], lats, lons)
    totals = None
    for quarter, value in (
        (2 * core + own, part),
        (2 * (1 - core) + beside, beside_part),
        (2 * core + 1 - own, other),
        (2 * (1 - core) + 1 - beside, beside_other),
    ):
        totals = place(quarter, value, taps, width, channels, loss_scale, totals)
    conv_total, encoder_total, gain_total = totals
    gain_total = gain_total[0]
    return (conv_out, conv_total.reshape(3, 3, width, width), encoder_total, gain_total)


def solution(mesh):
    placed = (
        P(("lat", "lon"), None),
        P(("lat", "lon")),
        P(("lat", "lon")),
        P(("lat", "lon")),
        P(),
        P(),
        P(),
        P(),
        P("lat", "lon", None),
    )

    return jax.shard_map(
        shards,
        mesh=mesh,
        in_specs=placed,
        out_specs=(P("lat", "lon", None), P(), P(), P()),
        check_vma=False,
    )
```

```python
import math

import jax
import jax.numpy as jnp
from jax import lax
from jax.experimental import pallas as pl
from jax.experimental.pallas import tpu as pltpu
from jax.sharding import PartitionSpec as P


PH = 8
PW = 16
MOST = 3
EPS = 1e-06
LANES = 128
AXES = ("lat", "lon")
VMEM_LIMIT = 24 * 1024 * 1024


def bits_of(count):
    assert count & (count - 1) == 0
    return [1 << i for i in range(count.bit_length() - 1)]


def parity(value, mask):
    out = jnp.zeros((), jnp.int32)
    while mask:
        low = mask & -mask
        out = out ^ ((value & low) != 0).astype(jnp.int32)
        mask ^= low
    return out


def exchange(value, lats, lons, move):
    pairs = []
    for a in range(lats):
        for b in range(lons):
            c, d = move(a, b)
            pairs.append((a * lons + b, c * lons + d))
    return lax.ppermute(value, AXES, pairs)


def stage_plan(lats, lons):
    lat_bits, lon_bits = bits_of(lats), bits_of(lons)
    first = lat_bits[:1]
    lat_rest = lat_bits[1:]
    low, high = lon_bits[:1], lon_bits[1:]
    plan = [(((m, 0), (m, 0)), ((m, 0), (m, 0))) for m in first]
    ab = [(m, 0) for m in lat_rest] + [(0, m) for m in low]
    ba = [(0, m) for m in low] + [(m, 0) for m in lat_rest]
    plan += [((p, q), (p, q)) for p, q in zip(ab, ba)]
    if len(high) == 2:
        one, two = high
        plan += [(((0, one),) * 2, ((0, one | two),) * 2), (((0, one | two),) * 2, ((0, two),) * 2)]
    else:
        plan += [(((0, m),) * 2, ((0, m),) * 2) for m in high]
    return plan


def kept_half(masks, lat, lon):
    even = parity(lat, masks[0][0]) ^ parity(lon, masks[0][1])
    odd = parity(lat, masks[1][0]) ^ parity(lon, masks[1][1])
    return jnp.where((lat & 1) == 0, even, odd)


def step(value, steps, lats, lons):
    return exchange(value, lats, lons, lambda a, b: (a ^ steps[a & 1][0], b ^ steps[a & 1][1]))


def pick(value, half):
    pair = value.reshape(2, value.shape[0] // 2, value.shape[1])
    return lax.dynamic_index_in_dim(pair, half, 0, keepdims=False)


def split_sum(keep, came, half):
    away = pick(keep, 1 - half) + pick(came, 1 - half).astype(jnp.float32)
    stay = pick(keep, half) + pick(came, half).astype(jnp.float32)
    return away.astype(jnp.bfloat16), stay


def padded_2(shard, sides, width, wrap):
    for axis, dim in sides:
        size, length = (lax.axis_size(axis), shard.shape[dim])
        up = [(i, (i + 1) % size) for i in range(size if wrap else size - 1)]
        down = [(j, i) for i, j in up]
        last = lax.slice_in_dim(shard, length - width, length, axis=dim)
        leading = lax.slice_in_dim(shard, 0, width, axis=dim)
        before = lax.ppermute(last, axis, up)
        after = lax.ppermute(leading, axis, down)
        shard = jnp.concatenate([before, shard, after], axis=dim)
    return shard


def to_patches(tile):
    rows, cols, width = tile.shape
    shaped = tile.reshape(rows // PH, PH, cols // PW, PW, width)
    return shaped.transpose(0, 2, 1, 3, 4).reshape(-1, width)


def whole(shape):
    zeros = (0,) * len(shape)
    return pl.BlockSpec(shape, lambda *_: zeros, pipeline_mode=pl.Buffered(1))


def call(body, scalars, ins, outs, grid=(1,), in_specs=None, out_specs=None, scratch=(), alias=None):
    return pl.pallas_call(
        body,
        out_shape=outs,
        grid_spec=pltpu.PrefetchScalarGridSpec(
            num_scalar_prefetch=1,
            grid=grid,
            in_specs=in_specs or [whole(a.shape) for a in ins],
            out_specs=out_specs or [whole(o.shape) for o in outs],
            scratch_shapes=list(scratch),
        ),
        input_output_aliases=alias or {},
        compiler_params=pltpu.CompilerParams(vmem_limit_bytes=VMEM_LIMIT),
    )(scalars, *ins)


def shape_of(shape, dtype):
    return jax.ShapeDtypeStruct(shape, dtype)


def nt(left, right):
    return lax.dot_general(left, right, (((1,), (1,)), ((), ())), preferred_element_type=jnp.float32)


def lanes(at, size):
    return pl.ds(pl.multiple_of(at * size, size), size)


def pack(spectra_t, source, places, rows):
    channels = spectra_t.shape[0]

    def body(src, full, *refs):
        outs, sems = refs[:-1], refs[-1]
        copies = []
        for n, k in enumerate(places):
            for j in range(MOST):
                copies.append(
                    pltpu.make_async_copy(
                        full.at[:, lanes(src[k * MOST + j], rows)],
                        outs[n].at[:, j * rows : (j + 1) * rows],
                        sems.at[n * MOST + j],
                    )
                )
        for c in copies:
            c.start()
        for c in copies:
            c.wait()

    outs = [shape_of((channels, MOST * rows), spectra_t.dtype)] * len(places)
    return call(
        body,
        source,
        [spectra_t],
        outs,
        in_specs=[pl.BlockSpec(memory_space=pl.ANY)],
        scratch=[pltpu.SemaphoreType.DMA((len(places) * MOST,))],
    )


def spread_blocks(meta, first, arrived, weight_t, kernels, gain_col, before, patches, last):
    count = len(arrived)
    kernel_count, rows, cells = kernels.shape
    width = weight_t.shape[0]

    def body(meta_ref, *refs):
        xs = refs[:count]
        w, kern, g = refs[count : count + 3]
        spread, slope, *rest = refs[count + 3 + (before is not None) :]
        if before is None:
            spread[...] = jnp.zeros_like(spread)
        else:
            spread[...] = refs[count + 3][...]
        for k in range(count):
            pre = jnp.dot(w[...], xs[k][...], preferred_element_type=jnp.float32)
            s = jax.nn.sigmoid(pre)
            slope[k] = (s * (1.0 + pre * (1.0 - s))).astype(jnp.bfloat16)
            enc = (pre * s).astype(jnp.bfloat16)
            for j in range(MOST):
                code = meta_ref[(first + k) * MOST + j]

                @pl.when(code >= 0)
                def _():
                    spread[code // kernel_count] += jnp.dot(
                        enc[:, j * rows : (j + 1) * rows],
                        kern[code % kernel_count],
                        preferred_element_type=jnp.float32,
                    )

        if last:
            for q in range(patches):
                cell = spread[q]
                r = lax.rsqrt(jnp.mean(cell * cell, axis=0, keepdims=True) + EPS)
                rest[0][:, q * cells : (q + 1) * cells] = (cell * r * g[...]).astype(jnp.bfloat16)

    outs = [
        shape_of((patches, width, cells), jnp.float32),
        shape_of((count, width, MOST * rows), jnp.bfloat16),
    ]
    if last:
        outs.append(shape_of((width, patches * cells), jnp.bfloat16))
    ins = [*arrived, weight_t, kernels, gain_col] + ([] if before is None else [before])
    return call(body, meta, ins, outs)


def backward(meta, arrived, kernels_t, gain_col, spread, slopes, d_normed_t):
    count = len(arrived)
    groups = len(slopes)
    place_of = [(n, k) for n, one in enumerate(slopes) for k in range(one.shape[0])]
    kernel_count, cells, rows = kernels_t.shape
    patches, width, _ = spread.shape
    channels = arrived[0].shape[0]

    def body(meta_ref, *refs):
        xs = refs[:count]
        slos = refs[count : count + groups]
        kern, g, spr, dn, out, dsp, dpre = refs[count + groups :]
        total = jnp.zeros((width, 1), jnp.float32)
        for q in range(patches):
            cell = spr[q]
            d = dn[:, q * cells : (q + 1) * cells]
            r = lax.rsqrt(jnp.mean(cell * cell, axis=0, keepdims=True) + EPS)
            unit = cell * r
            total = total + jnp.sum(d * unit, axis=1, keepdims=True)
            dg = d * g[...]
            inner = jnp.mean(dg * unit, axis=0, keepdims=True)
            dsp[q] = ((dg - unit * inner) * r).astype(jnp.bfloat16)
        out[...] = jnp.zeros_like(out)
        out[:, channels : channels + 1] = total
        for k in range(count):
            for j in range(MOST):
                code = meta_ref[k * MOST + j]
                span = slice(j * rows, (j + 1) * rows)

                @pl.when(code >= 0)
                def _():
                    drow = jnp.dot(
                        dsp[code // kernel_count],
                        kern[code % kernel_count],
                        preferred_element_type=jnp.float32,
                    ).astype(jnp.bfloat16)
                    dpre[:, span] = (
                        drow.astype(jnp.float32) * slos[place_of[k][0]][place_of[k][1], :, span].astype(jnp.float32)
                    ).astype(jnp.bfloat16)

                @pl.when(code < 0)
                def _():
                    dpre[:, span] = jnp.zeros((width, rows), jnp.bfloat16)

            out[:, :channels] += nt(dpre[...], xs[k][...])

    ins = [*arrived, *slopes, kernels_t, gain_col, spread, d_normed_t]
    outs = [shape_of((width, (channels // LANES + 1) * LANES), jnp.float32)]
    scratch = [
        pltpu.VMEM((patches, width, cells), jnp.bfloat16),
        pltpu.VMEM((width, MOST * rows), jnp.bfloat16),
    ]
    return call(body, meta, ins, outs, scratch=scratch)[0]


def place(quarter, part, taps, lane, channels, scale, into=None):
    rows = part.shape[0]
    steps = 2
    unit = rows // steps

    def body(at, piece, small, *refs):
        conv, encoder, gain = refs[-3:]
        for t in range(taps):
            conv[t] = piece[:, t * lane : (t + 1) * lane].astype(jnp.float32) * scale

        @pl.when(pl.program_id(0) == 0)
        def _():
            turned = (small[:, taps * lane :].astype(jnp.float32) * scale).T
            encoder[...] = turned[:channels]
            gain[...] = turned[channels : channels + 1]

    specs = [pl.BlockSpec((unit, part.shape[1]), lambda i, q: (i, 0)), whole(part.shape)]
    ins = [part, part]
    if into is not None:
        ins += list(into)
        specs += [pl.BlockSpec(memory_space=pl.ANY)] * 3
    return call(
        body,
        quarter.reshape(1),
        ins,
        [
            shape_of((taps, 4 * rows, lane), jnp.float32),
            shape_of((channels, 4 * rows), jnp.float32),
            shape_of((1, 4 * rows), jnp.float32),
        ],
        grid=(steps,),
        in_specs=specs,
        out_specs=[
            pl.BlockSpec((taps, unit, lane), lambda i, q: (0, q[0] * steps + i, 0)),
            pl.BlockSpec((channels, rows), lambda i, q: (0, q[0])),
            pl.BlockSpec((1, rows), lambda i, q: (0, q[0])),
        ],
        alias=None if into is None else {3: 0, 4: 1, 5: 2},
    )


def shards(
    spectra,
    block_target,
    block_patch,
    block_kernel,
    encoder_weight,
    kernels,
    gain,
    conv_weight,
    cotangent,
):
    lons = lax.axis_size("lon")
    lats = lax.axis_size("lat")
    lon = lax.axis_index("lon")
    blocks = block_target.shape[0]
    kernel_count, block_rows, _ = kernels.shape
    channels = spectra.shape[1]
    width = encoder_weight.shape[1]
    tile_rows, tile_cols = (cotangent.shape[0], cotangent.shape[1])
    loss_scale = 1.0 / math.sqrt(tile_rows * lats * tile_cols * lons)
    cells = tile_rows * tile_cols

    cot_beside = padded_2(cotangent, (("lon", 1),), 1, True)
    order = lon ^ jnp.arange(lons, dtype=jnp.int32)
    hit = (block_target[:, None] == order[None, :]).astype(jnp.int32)
    rank = jnp.cumsum(hit, axis=0) - hit
    chosen = hit[:, :, None] * (rank[:, :, None] == jnp.arange(MOST)[None, None, :]).astype(jnp.int32)
    number = jnp.arange(blocks, dtype=jnp.int32)
    source = jnp.sum(chosen * number[:, None, None], axis=0).reshape(-1)
    code = block_patch * kernel_count + block_kernel + 1
    codes = jnp.sum(chosen * code[:, None, None], axis=0) - 1
    spectra_t = spectra.T
    far, near = range(lons // 2, lons), range(lons // 2)
    packed = dict(zip(far, pack(spectra_t, source, far, block_rows)))
    packed |= zip(near, pack(spectra_t, source, near, block_rows))
    cot_padded = padded_2(cot_beside, (("lat", 0),), 1, False)

    by_tile = jnp.sum(
        jnp.where((order[None, :] == jnp.arange(lons)[:, None])[:, :, None], codes[None], 0), axis=1
    )
    came = lax.all_to_all(by_tile, "lon", 0, 0, tiled=True)
    meta = jnp.sum(
        jnp.where((order[:, None] == jnp.arange(lons)[None, :])[:, :, None], came[None], 0), axis=1
    ).reshape(-1)

    arrived = [packed[0]] + [None] * (lons - 1)
    for k in [*far, *near[1:]]:
        arrived[k] = exchange(packed[k], lats, lons, lambda a, b, k=k: (a, b ^ k))

    windows = jnp.concatenate(
        [
            to_patches(cot_padded[2 - a : 2 - a + tile_rows, 2 - b : 2 - b + tile_cols])
            for a in range(3)
            for b in range(3)
        ],
        axis=1,
    )
    taps = 9
    weight_all = conv_weight.reshape(taps, width, width).transpose(1, 0, 2).reshape(width, -1)
    d_normed_t = nt(weight_all, windows)

    meta, d_normed_t, windows = lax.optimization_barrier((meta, d_normed_t, windows))
    patches = tile_rows // PH * (tile_cols // PW)
    gain_col = gain.reshape(width, 1)
    weight_t = encoder_weight.T
    cuts = [0, lons // 2, lons - 1, lons]
    spread, slopes = None, []
    for low, high in zip(cuts, cuts[1:]):
        last = high == lons
        spread, slope, *rest = spread_blocks(
            meta, low, arrived[low:high], weight_t, kernels, gain_col, spread, patches, last
        )
        slopes.append(slope)
    normed_t = rest[0]

    plan = stage_plan(lats, lons)
    lat = lax.axis_index("lat")
    halves = [kept_half(masks, lat, lon) for _, masks in plan]
    core = halves[0]
    away = jnp.dot(
        pick(normed_t, 1 - core), windows, preferred_element_type=jnp.float32
    ).astype(jnp.bfloat16)
    keep = jnp.dot(pick(normed_t, core), windows, preferred_element_type=jnp.float32)
    came = step(away, plan[0][0], lats, lons)

    away, keep = split_sum(keep, came, halves[1])
    away, spread = lax.optimization_barrier((away, spread))
    came = step(away, plan[1][0], lats, lons)
    kernels_t = kernels.transpose(0, 2, 1)
    small = backward(meta, arrived, kernels_t, gain_col, spread, slopes, d_normed_t)
    small_keep = pick(small, core)
    small_came = step(pick(small, 1 - core).astype(jnp.bfloat16), plan[0][0], lats, lons)

    away, small_keep = split_sum(small_keep, small_came, halves[1])
    small_came = step(away, plan[1][0], lats, lons)
    apart = len(plan) - 2
    for n in range(2, apart):
        away, keep = split_sum(keep, came, halves[n])
        came = step(away, plan[n][0], lats, lons)
        away, small_keep = split_sum(small_keep, small_came, halves[n])
        small_came = step(away, plan[n][0], lats, lons)
    keep = jnp.concatenate([keep, small_keep], axis=1)
    came = jnp.concatenate([came, small_came], axis=1)
    for n in range(apart, len(plan)):
        away, keep = split_sum(keep, came, halves[n])
        came = step(away, plan[n][0], lats, lons)
    normed = normed_t.reshape(width, tile_rows // PH, tile_cols // PW, PH, PW)
    normed = normed.transpose(1, 3, 2, 4, 0).reshape(tile_rows, tile_cols, width)
    padded = padded_2(normed, (("lon", 1),), 1, True)
    padded = padded_2(padded, (("lat", 0),), 1, False)
    result_sum = jnp.zeros((cells, width), jnp.float32)
    for a in range(3):
        for b in range(3):
            window = padded[a : a + tile_rows, b : b + tile_cols].reshape(-1, width)
            result_sum = result_sum + jnp.dot(
                window, conv_weight[a, b], preferred_element_type=jnp.float32
            )
    conv_out = result_sum.reshape(tile_rows, tile_cols, width).astype(jnp.bfloat16)
    part = (keep + came.astype(jnp.float32)).astype(jnp.bfloat16)
    for n in range(len(plan) - 1, 1, -1):
        other = step(part, plan[n][0], lats, lons)
        part = jnp.where(
            halves[n] == 0, jnp.concatenate([part, other]), jnp.concatenate([other, part])
        )
    part, conv_out = lax.optimization_barrier((part, conv_out))
    own, beside = halves[1], kept_half(plan[1][1], lat ^ 1, lon)
    other = step(part, plan[1][0], lats, lons)
    beside_part = step(part, plan[0][0], lats, lons)
    beside_other = step(other, plan[0][0], lats, lons)
    totals = None
    for quarter, value in (
        (2 * core + own, part),
        (2 * (1 - core) + beside, beside_part),
        (2 * core + 1 - own, other),
        (2 * (1 - core) + 1 - beside, beside_other),
    ):
        totals = place(quarter, value, taps, width, channels, loss_scale, totals)
    conv_total, encoder_total, gain_total = totals
    gain_total = gain_total[0]
    return (conv_out, conv_total.reshape(3, 3, width, width), encoder_total, gain_total)


def solution(mesh):
    placed = (
        P(("lat", "lon"), None),
        P(("lat", "lon")),
        P(("lat", "lon")),
        P(("lat", "lon")),
        P(),
        P(),
        P(),
        P(),
        P("lat", "lon", None),
    )

    return jax.shard_map(
        shards,
        mesh=mesh,
        in_specs=placed,
        out_specs=(P("lat", "lon", None), P(), P(), P()),
        check_vma=False,
    )
```

```python
import math

import jax
import jax.numpy as jnp
from jax import lax
from jax.experimental import pallas as pl
from jax.experimental.pallas import tpu as pltpu
from jax.sharding import PartitionSpec as P


PH = 8
PW = 16
MOST = 3
EPS = 1e-06
LANES = 128
AXES = ("lat", "lon")
VMEM_LIMIT = 24 * 1024 * 1024


def bits_of(count):
    assert count & (count - 1) == 0
    return [1 << i for i in range(count.bit_length() - 1)]


def parity(value, mask):
    out = jnp.zeros((), jnp.int32)
    while mask:
        low = mask & -mask
        out = out ^ ((value & low) != 0).astype(jnp.int32)
        mask ^= low
    return out


def exchange(value, lats, lons, move):
    pairs = []
    for a in range(lats):
        for b in range(lons):
            c, d = move(a, b)
            pairs.append((a * lons + b, c * lons + d))
    return lax.ppermute(value, AXES, pairs)


def stage_plan(lats, lons):
    lat_bits, lon_bits = bits_of(lats), bits_of(lons)
    first = lat_bits[:1]
    lat_rest = lat_bits[1:]
    low, high = lon_bits[:1], lon_bits[1:]
    plan = [(((m, 0), (m, 0)), ((m, 0), (m, 0))) for m in first]
    ab = [(m, 0) for m in lat_rest] + [(0, m) for m in low]
    ba = [(0, m) for m in low] + [(m, 0) for m in lat_rest]
    plan += [((p, q), (p, q)) for p, q in zip(ab, ba)]
    if len(high) == 2:
        one, two = high
        plan += [(((0, one),) * 2, ((0, one | two),) * 2), (((0, one | two),) * 2, ((0, two),) * 2)]
    else:
        plan += [(((0, m),) * 2, ((0, m),) * 2) for m in high]
    return plan


def kept_half(masks, lat, lon):
    even = parity(lat, masks[0][0]) ^ parity(lon, masks[0][1])
    odd = parity(lat, masks[1][0]) ^ parity(lon, masks[1][1])
    return jnp.where((lat & 1) == 0, even, odd)


def step(value, steps, lats, lons):
    return exchange(value, lats, lons, lambda a, b: (a ^ steps[a & 1][0], b ^ steps[a & 1][1]))


def pick(value, half):
    pair = value.reshape(2, value.shape[0] // 2, value.shape[1])
    return lax.dynamic_index_in_dim(pair, half, 0, keepdims=False)


def split_sum(keep, came, half):
    away = pick(keep, 1 - half) + pick(came, 1 - half).astype(jnp.float32)
    stay = pick(keep, half) + pick(came, half).astype(jnp.float32)
    return away.astype(jnp.bfloat16), stay


def padded_2(shard, sides, width, wrap):
    for axis, dim in sides:
        size, length = (lax.axis_size(axis), shard.shape[dim])
        up = [(i, (i + 1) % size) for i in range(size if wrap else size - 1)]
        down = [(j, i) for i, j in up]
        last = lax.slice_in_dim(shard, length - width, length, axis=dim)
        leading = lax.slice_in_dim(shard, 0, width, axis=dim)
        before = lax.ppermute(last, axis, up)
        after = lax.ppermute(leading, axis, down)
        shard = jnp.concatenate([before, shard, after], axis=dim)
    return shard


def to_patches(tile):
    rows, cols, width = tile.shape
    shaped = tile.reshape(rows // PH, PH, cols // PW, PW, width)
    return shaped.transpose(0, 2, 1, 3, 4).reshape(-1, width)


def whole(shape):
    zeros = (0,) * len(shape)
    return pl.BlockSpec(shape, lambda *_: zeros, pipeline_mode=pl.Buffered(1))


def call(body, scalars, ins, outs, grid=(1,), in_specs=None, out_specs=None, scratch=(), alias=None):
    return pl.pallas_call(
        body,
        out_shape=outs,
        grid_spec=pltpu.PrefetchScalarGridSpec(
            num_scalar_prefetch=1,
            grid=grid,
            in_specs=in_specs or [whole(a.shape) for a in ins],
            out_specs=out_specs or [whole(o.shape) for o in outs],
            scratch_shapes=list(scratch),
        ),
        input_output_aliases=alias or {},
        compiler_params=pltpu.CompilerParams(vmem_limit_bytes=VMEM_LIMIT),
    )(scalars, *ins)


def shape_of(shape, dtype):
    return jax.ShapeDtypeStruct(shape, dtype)


def nt(left, right):
    return lax.dot_general(left, right, (((1,), (1,)), ((), ())), preferred_element_type=jnp.float32)


def lanes(at, size):
    return pl.ds(pl.multiple_of(at * size, size), size)


def pack(spectra_t, source, places, rows):
    channels = spectra_t.shape[0]

    def body(src, full, *refs):
        outs, sems = refs[:-1], refs[-1]
        copies = []
        for n, k in enumerate(places):
            for j in range(MOST):
                copies.append(
                    pltpu.make_async_copy(
                        full.at[:, lanes(src[k * MOST + j], rows)],
                        outs[n].at[:, j * rows : (j + 1) * rows],
                        sems.at[n * MOST + j],
                    )
                )
        for c in copies:
            c.start()
        for c in copies:
            c.wait()

    outs = [shape_of((channels, MOST * rows), spectra_t.dtype)] * len(places)
    return call(
        body,
        source,
        [spectra_t],
        outs,
        in_specs=[pl.BlockSpec(memory_space=pl.ANY)],
        scratch=[pltpu.SemaphoreType.DMA((len(places) * MOST,))],
    )


def spread_blocks(meta, first, arrived, weight_t, kernels, gain_col, before, patches, last):
    count = len(arrived)
    kernel_count, rows, cells = kernels.shape
    width = weight_t.shape[0]

    def body(meta_ref, *refs):
        xs = refs[:count]
        w, kern, g = refs[count : count + 3]
        spread, slope, *rest, enc = refs[count + 3 + (before is not None) :]
        if before is None:
            spread[...] = jnp.zeros_like(spread)
        else:
            spread[...] = refs[count + 3][...]
        for k in range(count):
            pre = jnp.dot(w[...], xs[k][...], preferred_element_type=jnp.float32)
            s = jax.nn.sigmoid(pre)
            slope[k] = (s * (1.0 + pre * (1.0 - s))).astype(jnp.bfloat16)
            enc[...] = (pre * s).astype(jnp.bfloat16)

            def add(j, _, k=k):
                code = meta_ref[(first + k) * MOST + j]

                @pl.when(code >= 0)
                def _():
                    spread[code // kernel_count] += jnp.dot(
                        enc[:, lanes(j, rows)],
                        kern[code % kernel_count],
                        preferred_element_type=jnp.float32,
                    )

                return 0

            lax.fori_loop(0, MOST, add, 0)

        if last:

            def norm(q, _):
                cell = spread[q]
                r = lax.rsqrt(jnp.mean(cell * cell, axis=0, keepdims=True) + EPS)
                rest[0][:, lanes(q, cells)] = (cell * r * g[...]).astype(jnp.bfloat16)
                return 0

            lax.fori_loop(0, patches, norm, 0)

    outs = [
        shape_of((patches, width, cells), jnp.float32),
        shape_of((count, width, MOST * rows), jnp.bfloat16),
    ]
    if last:
        outs.append(shape_of((width, patches * cells), jnp.bfloat16))
    ins = [*arrived, weight_t, kernels, gain_col] + ([] if before is None else [before])
    scratch = [pltpu.VMEM((width, MOST * rows), jnp.bfloat16)]
    return call(body, meta, ins, outs, scratch=scratch)


def backward(meta, arrived, kernels_t, gain_col, spread, slopes, d_normed_t):
    count = len(arrived)
    groups = len(slopes)
    place_of = [(n, k) for n, one in enumerate(slopes) for k in range(one.shape[0])]
    kernel_count, cells, rows = kernels_t.shape
    patches, width, _ = spread.shape
    channels = arrived[0].shape[0]

    def body(meta_ref, *refs):
        xs = refs[:count]
        slos = refs[count : count + groups]
        kern, g, spr, dn, out, dsp, dpre = refs[count + groups :]

        def unnorm(q, total):
            cell = spr[q]
            d = dn[:, lanes(q, cells)]
            r = lax.rsqrt(jnp.mean(cell * cell, axis=0, keepdims=True) + EPS)
            unit = cell * r
            dg = d * g[...]
            inner = jnp.mean(dg * unit, axis=0, keepdims=True)
            dsp[q] = ((dg - unit * inner) * r).astype(jnp.bfloat16)
            return total + jnp.sum(d * unit, axis=1, keepdims=True)

        total = lax.fori_loop(0, patches, unnorm, jnp.zeros((width, 1), jnp.float32))
        out[...] = jnp.zeros_like(out)
        out[:, channels : channels + 1] = total
        for k in range(count):
            n, at = place_of[k]

            def back(j, _, k=k, n=n, at=at):
                code = meta_ref[k * MOST + j]
                span = lanes(j, rows)

                @pl.when(code >= 0)
                def _():
                    drow = jnp.dot(
                        dsp[code // kernel_count],
                        kern[code % kernel_count],
                        preferred_element_type=jnp.float32,
                    ).astype(jnp.bfloat16)
                    dpre[:, span] = (
                        drow.astype(jnp.float32) * slos[n][at, :, span].astype(jnp.float32)
                    ).astype(jnp.bfloat16)

                @pl.when(code < 0)
                def _():
                    dpre[:, span] = jnp.zeros((width, rows), jnp.bfloat16)

                return 0

            lax.fori_loop(0, MOST, back, 0)
            out[:, :channels] += nt(dpre[...], xs[k][...])

    ins = [*arrived, *slopes, kernels_t, gain_col, spread, d_normed_t]
    outs = [shape_of((width, (channels // LANES + 1) * LANES), jnp.float32)]
    scratch = [
        pltpu.VMEM((patches, width, cells), jnp.bfloat16),
        pltpu.VMEM((width, MOST * rows), jnp.bfloat16),
    ]
    return call(body, meta, ins, outs, scratch=scratch)[0]


def place(quarter, part, taps, lane, channels, scale, into=None):
    rows = part.shape[0]
    steps = 2
    unit = rows // steps

    def body(at, piece, small, *refs):
        conv, encoder, gain = refs[-3:]
        for t in range(taps):
            conv[t] = piece[:, t * lane : (t + 1) * lane].astype(jnp.float32) * scale

        @pl.when(pl.program_id(0) == 0)
        def _():
            turned = (small[:, taps * lane :].astype(jnp.float32) * scale).T
            encoder[...] = turned[:channels]
            gain[...] = turned[channels : channels + 1]

    specs = [pl.BlockSpec((unit, part.shape[1]), lambda i, q: (i, 0)), whole(part.shape)]
    ins = [part, part]
    if into is not None:
        ins += list(into)
        specs += [pl.BlockSpec(memory_space=pl.ANY)] * 3
    return call(
        body,
        quarter.reshape(1),
        ins,
        [
            shape_of((taps, 4 * rows, lane), jnp.float32),
            shape_of((channels, 4 * rows), jnp.float32),
            shape_of((1, 4 * rows), jnp.float32),
        ],
        grid=(steps,),
        in_specs=specs,
        out_specs=[
            pl.BlockSpec((taps, unit, lane), lambda i, q: (0, q[0] * steps + i, 0)),
            pl.BlockSpec((channels, rows), lambda i, q: (0, q[0])),
            pl.BlockSpec((1, rows), lambda i, q: (0, q[0])),
        ],
        alias=None if into is None else {3: 0, 4: 1, 5: 2},
    )


def shards(
    spectra,
    block_target,
    block_patch,
    block_kernel,
    encoder_weight,
    kernels,
    gain,
    conv_weight,
    cotangent,
):
    lons = lax.axis_size("lon")
    lats = lax.axis_size("lat")
    lon = lax.axis_index("lon")
    blocks = block_target.shape[0]
    kernel_count, block_rows, _ = kernels.shape
    channels = spectra.shape[1]
    width = encoder_weight.shape[1]
    tile_rows, tile_cols = (cotangent.shape[0], cotangent.shape[1])
    loss_scale = 1.0 / math.sqrt(tile_rows * lats * tile_cols * lons)
    cells = tile_rows * tile_cols

    cot_beside = padded_2(cotangent, (("lon", 1),), 1, True)
    order = lon ^ jnp.arange(lons, dtype=jnp.int32)
    hit = (block_target[:, None] == order[None, :]).astype(jnp.int32)
    rank = jnp.cumsum(hit, axis=0) - hit
    chosen = hit[:, :, None] * (rank[:, :, None] == jnp.arange(MOST)[None, None, :]).astype(jnp.int32)
    number = jnp.arange(blocks, dtype=jnp.int32)
    source = jnp.sum(chosen * number[:, None, None], axis=0).reshape(-1)
    code = block_patch * kernel_count + block_kernel + 1
    codes = jnp.sum(chosen * code[:, None, None], axis=0) - 1
    spectra_t = spectra.T
    far, near = range(lons // 2, lons), range(lons // 2)
    packed = dict(zip(far, pack(spectra_t, source, far, block_rows)))
    packed |= zip(near, pack(spectra_t, source, near, block_rows))
    cot_padded = padded_2(cot_beside, (("lat", 0),), 1, False)

    by_tile = jnp.sum(
        jnp.where((order[None, :] == jnp.arange(lons)[:, None])[:, :, None], codes[None], 0), axis=1
    )
    came = lax.all_to_all(by_tile, "lon", 0, 0, tiled=True)
    meta = jnp.sum(
        jnp.where((order[:, None] == jnp.arange(lons)[None, :])[:, :, None], came[None], 0), axis=1
    ).reshape(-1)

    arrived = [packed[0]] + [None] * (lons - 1)
    for k in [*far, *near[1:]]:
        arrived[k] = exchange(packed[k], lats, lons, lambda a, b, k=k: (a, b ^ k))

    windows = jnp.concatenate(
        [
            to_patches(cot_padded[2 - a : 2 - a + tile_rows, 2 - b : 2 - b + tile_cols])
            for a in range(3)
            for b in range(3)
        ],
        axis=1,
    )
    taps = 9
    weight_all = conv_weight.reshape(taps, width, width).transpose(1, 0, 2).reshape(width, -1)
    d_normed_t = nt(weight_all, windows)

    meta, d_normed_t, windows = lax.optimization_barrier((meta, d_normed_t, windows))
    patches = tile_rows // PH * (tile_cols // PW)
    gain_col = gain.reshape(width, 1)
    weight_t = encoder_weight.T
    cuts = [0, lons // 2, lons - 1, lons]
    spread, slopes = None, []
    for low, high in zip(cuts, cuts[1:]):
        last = high == lons
        spread, slope, *rest = spread_blocks(
            meta, low, arrived[low:high], weight_t, kernels, gain_col, spread, patches, last
        )
        slopes.append(slope)
    normed_t = rest[0]

    plan = stage_plan(lats, lons)
    lat = lax.axis_index("lat")
    halves = [kept_half(masks, lat, lon) for _, masks in plan]
    core = halves[0]
    away = jnp.dot(
        pick(normed_t, 1 - core), windows, preferred_element_type=jnp.float32
    ).astype(jnp.bfloat16)
    keep = jnp.dot(pick(normed_t, core), windows, preferred_element_type=jnp.float32)
    came = step(away, plan[0][0], lats, lons)

    away, keep = split_sum(keep, came, halves[1])
    away, spread, normed_after = lax.optimization_barrier((away, spread, normed_t))
    came = step(away, plan[1][0], lats, lons)
    kernels_t = kernels.transpose(0, 2, 1)
    small = backward(meta, arrived, kernels_t, gain_col, spread, slopes, d_normed_t)
    small_keep = pick(small, core)
    small_came = step(pick(small, 1 - core).astype(jnp.bfloat16), plan[0][0], lats, lons)

    away, small_keep = split_sum(small_keep, small_came, halves[1])
    small_came = step(away, plan[1][0], lats, lons)
    apart = len(plan) - 2
    for n in range(2, apart):
        away, keep = split_sum(keep, came, halves[n])
        came = step(away, plan[n][0], lats, lons)
        away, small_keep = split_sum(small_keep, small_came, halves[n])
        small_came = step(away, plan[n][0], lats, lons)
    keep = jnp.concatenate([keep, small_keep], axis=1)
    came = jnp.concatenate([came, small_came], axis=1)
    for n in range(apart, len(plan)):
        away, keep = split_sum(keep, came, halves[n])
        came = step(away, plan[n][0], lats, lons)
    normed = normed_after.reshape(width, tile_rows // PH, tile_cols // PW, PH, PW)
    normed = normed.transpose(1, 3, 2, 4, 0).reshape(tile_rows, tile_cols, width)
    padded = padded_2(normed, (("lon", 1),), 1, True)
    padded = padded_2(padded, (("lat", 0),), 1, False)
    result_sum = jnp.zeros((cells, width), jnp.float32)
    for a in range(3):
        for b in range(3):
            window = padded[a : a + tile_rows, b : b + tile_cols].reshape(-1, width)
            result_sum = result_sum + jnp.dot(
                window, conv_weight[a, b], preferred_element_type=jnp.float32
            )
    conv_out = result_sum.reshape(tile_rows, tile_cols, width).astype(jnp.bfloat16)
    part = (keep + came.astype(jnp.float32)).astype(jnp.bfloat16)
    for n in range(len(plan) - 1, 1, -1):
        other = step(part, plan[n][0], lats, lons)
        part = jnp.where(
            halves[n] == 0, jnp.concatenate([part, other]), jnp.concatenate([other, part])
        )
    own, beside = halves[1], kept_half(plan[1][1], lat ^ 1, lon)
    other = step(part, plan[1][0], lats, lons)
    beside_part = step(part, plan[0][0], lats, lons)
    beside_other = step(other, plan[0][0], lats, lons)
    totals = None
    for quarter, value in (
        (2 * core + own, part),
        (2 * (1 - core) + beside, beside_part),
        (2 * core + 1 - own, other),
        (2 * (1 - core) + 1 - beside, beside_other),
    ):
        totals = place(quarter, value, taps, width, channels, loss_scale, totals)
    conv_total, encoder_total, gain_total = totals
    gain_total = gain_total[0]
    return (conv_out, conv_total.reshape(3, 3, width, width), encoder_total, gain_total)


def solution(mesh):
    placed = (
        P(("lat", "lon"), None),
        P(("lat", "lon")),
        P(("lat", "lon")),
        P(("lat", "lon")),
        P(),
        P(),
        P(),
        P(),
        P("lat", "lon", None),
    )

    return jax.shard_map(
        shards,
        mesh=mesh,
        in_specs=placed,
        out_specs=(P("lat", "lon", None), P(), P(), P()),
        check_vma=False,
    )
```

```python
import math

import jax
import jax.numpy as jnp
from jax import lax
from jax.experimental import pallas as pl
from jax.experimental.pallas import tpu as pltpu
from jax.sharding import PartitionSpec as P


PH = 8
PW = 16
MOST = 3
EPS = 1e-06
LANES = 128
AXES = ("lat", "lon")
VMEM_LIMIT = 24 * 1024 * 1024


def bits_of(count):
    assert count & (count - 1) == 0
    return [1 << i for i in range(count.bit_length() - 1)]


def parity(value, mask):
    out = jnp.zeros((), jnp.int32)
    while mask:
        low = mask & -mask
        out = out ^ ((value & low) != 0).astype(jnp.int32)
        mask ^= low
    return out


def exchange(value, lats, lons, move):
    pairs = []
    for a in range(lats):
        for b in range(lons):
            c, d = move(a, b)
            pairs.append((a * lons + b, c * lons + d))
    return lax.ppermute(value, AXES, pairs)


def stage_plan(lats, lons):
    lat_bits, lon_bits = bits_of(lats), bits_of(lons)
    first = lat_bits[:1]
    lat_rest = lat_bits[1:]
    low, high = lon_bits[:1], lon_bits[1:]
    plan = [(((m, 0), (m, 0)), ((m, 0), (m, 0))) for m in first]
    ab = [(m, 0) for m in lat_rest] + [(0, m) for m in low]
    ba = [(0, m) for m in low] + [(m, 0) for m in lat_rest]
    plan += [((p, q), (p, q)) for p, q in zip(ab, ba)]
    if len(high) == 2:
        one, two = high
        plan += [(((0, one),) * 2, ((0, one | two),) * 2), (((0, one | two),) * 2, ((0, two),) * 2)]
    else:
        plan += [(((0, m),) * 2, ((0, m),) * 2) for m in high]
    return plan


def kept_half(masks, lat, lon):
    even = parity(lat, masks[0][0]) ^ parity(lon, masks[0][1])
    odd = parity(lat, masks[1][0]) ^ parity(lon, masks[1][1])
    return jnp.where((lat & 1) == 0, even, odd)


def step(value, steps, lats, lons):
    return exchange(value, lats, lons, lambda a, b: (a ^ steps[a & 1][0], b ^ steps[a & 1][1]))


def pick(value, half):
    pair = value.reshape(2, value.shape[0] // 2, value.shape[1])
    return lax.dynamic_index_in_dim(pair, half, 0, keepdims=False)


def split_sum(keep, came, half):
    away = pick(keep, 1 - half) + pick(came, 1 - half).astype(jnp.float32)
    stay = pick(keep, half) + pick(came, half).astype(jnp.float32)
    return away.astype(jnp.bfloat16), stay


def padded_2(shard, sides, width, wrap):
    for axis, dim in sides:
        size, length = (lax.axis_size(axis), shard.shape[dim])
        up = [(i, (i + 1) % size) for i in range(size if wrap else size - 1)]
        down = [(j, i) for i, j in up]
        last = lax.slice_in_dim(shard, length - width, length, axis=dim)
        leading = lax.slice_in_dim(shard, 0, width, axis=dim)
        before = lax.ppermute(last, axis, up)
        after = lax.ppermute(leading, axis, down)
        shard = jnp.concatenate([before, shard, after], axis=dim)
    return shard


def to_patches(tile):
    rows, cols, width = tile.shape
    shaped = tile.reshape(rows // PH, PH, cols // PW, PW, width)
    return shaped.transpose(0, 2, 1, 3, 4).reshape(-1, width)


def whole(shape):
    zeros = (0,) * len(shape)
    return pl.BlockSpec(shape, lambda *_: zeros, pipeline_mode=pl.Buffered(1))


def call(body, scalars, ins, outs, grid=(1,), in_specs=None, out_specs=None, scratch=(), alias=None):
    return pl.pallas_call(
        body,
        out_shape=outs,
        grid_spec=pltpu.PrefetchScalarGridSpec(
            num_scalar_prefetch=1,
            grid=grid,
            in_specs=in_specs or [whole(a.shape) for a in ins],
            out_specs=out_specs or [whole(o.shape) for o in outs],
            scratch_shapes=list(scratch),
        ),
        input_output_aliases=alias or {},
        compiler_params=pltpu.CompilerParams(vmem_limit_bytes=VMEM_LIMIT),
    )(scalars, *ins)


def shape_of(shape, dtype):
    return jax.ShapeDtypeStruct(shape, dtype)


def nt(left, right):
    return lax.dot_general(left, right, (((1,), (1,)), ((), ())), preferred_element_type=jnp.float32)


def lanes(at, size):
    return pl.ds(pl.multiple_of(at * size, size), size)


def pack(spectra_t, source, places, rows):
    channels = spectra_t.shape[0]

    def body(src, full, *refs):
        outs, sems = refs[:-1], refs[-1]
        copies = []
        for n, k in enumerate(places):
            for j in range(MOST):
                copies.append(
                    pltpu.make_async_copy(
                        full.at[:, lanes(src[k * MOST + j], rows)],
                        outs[n].at[:, j * rows : (j + 1) * rows],
                        sems.at[n * MOST + j],
                    )
                )
        for c in copies:
            c.start()
        for c in copies:
            c.wait()

    outs = [shape_of((channels, MOST * rows), spectra_t.dtype)] * len(places)
    return call(
        body,
        source,
        [spectra_t],
        outs,
        in_specs=[pl.BlockSpec(memory_space=pl.ANY)],
        scratch=[pltpu.SemaphoreType.DMA((len(places) * MOST,))],
    )


def spread_blocks(meta, first, arrived, weight_t, kernels, gain_col, before, patches, last):
    count = len(arrived)
    kernel_count, rows, cells = kernels.shape
    width = weight_t.shape[0]

    def body(meta_ref, *refs):
        xs = refs[:count]
        w, kern, g = refs[count : count + 3]
        spread, slope, *rest, enc = refs[count + 3 + (before is not None) :]
        if before is None:
            spread[...] = jnp.zeros_like(spread)
        else:
            spread[...] = refs[count + 3][...]
        for k in range(count):
            pre = jnp.dot(w[...], xs[k][...], preferred_element_type=jnp.float32)
            s = jax.nn.sigmoid(pre)
            slope[k] = (s * (1.0 + pre * (1.0 - s))).astype(jnp.bfloat16)
            enc[...] = (pre * s).astype(jnp.bfloat16)

            def add(j, _, k=k):
                code = meta_ref[(first + k) * MOST + j]

                @pl.when(code >= 0)
                def _():
                    spread[code // kernel_count] += jnp.dot(
                        enc[:, lanes(j, rows)],
                        kern[code % kernel_count],
                        preferred_element_type=jnp.float32,
                    )

                return 0

            lax.fori_loop(0, MOST, add, 0)

        if last:

            def norm(q, _):
                cell = spread[q]
                r = lax.rsqrt(jnp.mean(cell * cell, axis=0, keepdims=True) + EPS)
                rest[0][:, lanes(q, cells)] = (cell * r * g[...]).astype(jnp.bfloat16)
                return 0

            lax.fori_loop(0, patches, norm, 0)

    outs = [
        shape_of((patches, width, cells), jnp.float32),
        shape_of((count, width, MOST * rows), jnp.bfloat16),
    ]
    if last:
        outs.append(shape_of((width, patches * cells), jnp.bfloat16))
    ins = [*arrived, weight_t, kernels, gain_col] + ([] if before is None else [before])
    scratch = [pltpu.VMEM((width, MOST * rows), jnp.bfloat16)]
    return call(body, meta, ins, outs, scratch=scratch)


def backward(meta, arrived, kernels_t, gain_col, spread, slopes, d_normed_t):
    count = len(arrived)
    groups = len(slopes)
    place_of = [(n, k) for n, one in enumerate(slopes) for k in range(one.shape[0])]
    kernel_count, cells, rows = kernels_t.shape
    patches, width, _ = spread.shape
    channels = arrived[0].shape[0]

    def body(meta_ref, *refs):
        xs = refs[:count]
        slos = refs[count : count + groups]
        kern, g, spr, dn, out, dsp, dpre, xbuf, sbuf, sems = refs[count + groups :]
        copies = []
        for k in range(count):
            n, at = place_of[k]
            copies.append(pltpu.make_async_copy(xs[k], xbuf.at[k], sems.at[2 * k]))
            copies.append(pltpu.make_async_copy(slos[n].at[at], sbuf.at[k], sems.at[2 * k + 1]))
        for one in copies:
            one.start()

        def unnorm(q, total):
            cell = spr[q]
            d = dn[:, lanes(q, cells)]
            r = lax.rsqrt(jnp.mean(cell * cell, axis=0, keepdims=True) + EPS)
            unit = cell * r
            dg = d * g[...]
            inner = jnp.mean(dg * unit, axis=0, keepdims=True)
            dsp[q] = ((dg - unit * inner) * r).astype(jnp.bfloat16)
            return total + jnp.sum(d * unit, axis=1, keepdims=True)

        total = lax.fori_loop(0, patches, unnorm, jnp.zeros((width, 1), jnp.float32))
        out[...] = jnp.zeros_like(out)
        out[:, channels : channels + 1] = total
        for k in range(count):
            copies[2 * k].wait()
            copies[2 * k + 1].wait()

            def back(j, _, k=k):
                code = meta_ref[k * MOST + j]
                span = lanes(j, rows)

                @pl.when(code >= 0)
                def _():
                    drow = jnp.dot(
                        dsp[code // kernel_count],
                        kern[code % kernel_count],
                        preferred_element_type=jnp.float32,
                    ).astype(jnp.bfloat16)
                    dpre[:, span] = (
                        drow.astype(jnp.float32) * sbuf[k, :, span].astype(jnp.float32)
                    ).astype(jnp.bfloat16)

                @pl.when(code < 0)
                def _():
                    dpre[:, span] = jnp.zeros((width, rows), jnp.bfloat16)

                return 0

            lax.fori_loop(0, MOST, back, 0)
            out[:, :channels] += nt(dpre[...], xbuf[k])

    ins = [*arrived, *slopes, kernels_t, gain_col, spread, d_normed_t]
    outs = [shape_of((width, (channels // LANES + 1) * LANES), jnp.float32)]
    scratch = [
        pltpu.VMEM((patches, width, cells), jnp.bfloat16),
        pltpu.VMEM((width, MOST * rows), jnp.bfloat16),
        pltpu.VMEM((count, channels, MOST * rows), jnp.bfloat16),
        pltpu.VMEM((count, width, MOST * rows), jnp.bfloat16),
        pltpu.SemaphoreType.DMA((2 * count,)),
    ]
    far = [pl.BlockSpec(memory_space=pl.ANY)] * (count + groups)
    in_specs = far + [whole(a.shape) for a in ins[count + groups :]]
    return call(body, meta, ins, outs, in_specs=in_specs, scratch=scratch)[0]


def place(quarter, part, taps, lane, channels, scale, into=None):
    rows = part.shape[0]
    steps = 2
    unit = rows // steps

    def body(at, piece, small, *refs):
        conv, encoder, gain = refs[-3:]
        for t in range(taps):
            conv[t] = piece[:, t * lane : (t + 1) * lane].astype(jnp.float32) * scale

        @pl.when(pl.program_id(0) == 0)
        def _():
            turned = (small[:, taps * lane :].astype(jnp.float32) * scale).T
            encoder[...] = turned[:channels]
            gain[...] = turned[channels : channels + 1]

    specs = [pl.BlockSpec((unit, part.shape[1]), lambda i, q: (i, 0)), whole(part.shape)]
    ins = [part, part]
    if into is not None:
        ins += list(into)
        specs += [pl.BlockSpec(memory_space=pl.ANY)] * 3
    return call(
        body,
        quarter.reshape(1),
        ins,
        [
            shape_of((taps, 4 * rows, lane), jnp.float32),
            shape_of((channels, 4 * rows), jnp.float32),
            shape_of((1, 4 * rows), jnp.float32),
        ],
        grid=(steps,),
        in_specs=specs,
        out_specs=[
            pl.BlockSpec((taps, unit, lane), lambda i, q: (0, q[0] * steps + i, 0)),
            pl.BlockSpec((channels, rows), lambda i, q: (0, q[0])),
            pl.BlockSpec((1, rows), lambda i, q: (0, q[0])),
        ],
        alias=None if into is None else {3: 0, 4: 1, 5: 2},
    )


def shards(
    spectra,
    block_target,
    block_patch,
    block_kernel,
    encoder_weight,
    kernels,
    gain,
    conv_weight,
    cotangent,
):
    lons = lax.axis_size("lon")
    lats = lax.axis_size("lat")
    lon = lax.axis_index("lon")
    blocks = block_target.shape[0]
    kernel_count, block_rows, _ = kernels.shape
    channels = spectra.shape[1]
    width = encoder_weight.shape[1]
    tile_rows, tile_cols = (cotangent.shape[0], cotangent.shape[1])
    loss_scale = 1.0 / math.sqrt(tile_rows * lats * tile_cols * lons)
    cells = tile_rows * tile_cols

    cot_beside = padded_2(cotangent, (("lon", 1),), 1, True)
    order = lon ^ jnp.arange(lons, dtype=jnp.int32)
    hit = (block_target[:, None] == order[None, :]).astype(jnp.int32)
    rank = jnp.cumsum(hit, axis=0) - hit
    chosen = hit[:, :, None] * (rank[:, :, None] == jnp.arange(MOST)[None, None, :]).astype(jnp.int32)
    number = jnp.arange(blocks, dtype=jnp.int32)
    source = jnp.sum(chosen * number[:, None, None], axis=0).reshape(-1)
    code = block_patch * kernel_count + block_kernel + 1
    codes = jnp.sum(chosen * code[:, None, None], axis=0) - 1
    spectra_t = spectra.T
    far, near = range(lons // 2, lons), range(lons // 2)
    packed = dict(zip(far, pack(spectra_t, source, far, block_rows)))
    packed |= zip(near, pack(spectra_t, source, near, block_rows))
    cot_padded = padded_2(cot_beside, (("lat", 0),), 1, False)

    by_tile = jnp.sum(
        jnp.where((order[None, :] == jnp.arange(lons)[:, None])[:, :, None], codes[None], 0), axis=1
    )
    came = lax.all_to_all(by_tile, "lon", 0, 0, tiled=True)
    meta = jnp.sum(
        jnp.where((order[:, None] == jnp.arange(lons)[None, :])[:, :, None], came[None], 0), axis=1
    ).reshape(-1)

    arrived = [packed[0]] + [None] * (lons - 1)
    for k in [*far, *near[1:]]:
        arrived[k] = exchange(packed[k], lats, lons, lambda a, b, k=k: (a, b ^ k))

    windows = jnp.concatenate(
        [
            to_patches(cot_padded[2 - a : 2 - a + tile_rows, 2 - b : 2 - b + tile_cols])
            for a in range(3)
            for b in range(3)
        ],
        axis=1,
    )
    taps = 9
    weight_all = conv_weight.reshape(taps, width, width).transpose(1, 0, 2).reshape(width, -1)
    d_normed_t = nt(weight_all, windows)

    meta, d_normed_t, windows = lax.optimization_barrier((meta, d_normed_t, windows))
    patches = tile_rows // PH * (tile_cols // PW)
    gain_col = gain.reshape(width, 1)
    weight_t = encoder_weight.T
    cuts = [0, lons // 2, lons - 1, lons]
    spread, slopes = None, []
    for low, high in zip(cuts, cuts[1:]):
        last = high == lons
        spread, slope, *rest = spread_blocks(
            meta, low, arrived[low:high], weight_t, kernels, gain_col, spread, patches, last
        )
        slopes.append(slope)
    normed_t = rest[0]

    plan = stage_plan(lats, lons)
    lat = lax.axis_index("lat")
    halves = [kept_half(masks, lat, lon) for _, masks in plan]
    core = halves[0]
    away = jnp.dot(
        pick(normed_t, 1 - core), windows, preferred_element_type=jnp.float32
    ).astype(jnp.bfloat16)
    came = step(away, plan[0][0], lats, lons)
    kernels_t = kernels.transpose(0, 2, 1)
    small = backward(meta, arrived, kernels_t, gain_col, spread, slopes, d_normed_t)
    small_came = step(pick(small, 1 - core).astype(jnp.bfloat16), plan[0][0], lats, lons)
    keep = jnp.dot(pick(normed_t, core), windows, preferred_element_type=jnp.float32)
    big_split = split_sum(keep, came, halves[1])
    small_split = split_sum(pick(small, core), small_came, halves[1])
    away, keep = [jnp.concatenate(both, axis=1) for both in zip(big_split, small_split)]
    away, normed_after = lax.optimization_barrier((away, normed_t))
    came = step(away, plan[1][0], lats, lons)
    for n in range(2, len(plan)):
        away, keep = split_sum(keep, came, halves[n])
        came = step(away, plan[n][0], lats, lons)
    normed = normed_after.reshape(width, tile_rows // PH, tile_cols // PW, PH, PW)
    normed = normed.transpose(1, 3, 2, 4, 0).reshape(tile_rows, tile_cols, width)
    padded = padded_2(normed, (("lon", 1),), 1, True)
    padded = padded_2(padded, (("lat", 0),), 1, False)
    result_sum = jnp.zeros((cells, width), jnp.float32)
    for a in range(3):
        for b in range(3):
            window = padded[a : a + tile_rows, b : b + tile_cols].reshape(-1, width)
            result_sum = result_sum + jnp.dot(
                window, conv_weight[a, b], preferred_element_type=jnp.float32
            )
        if a == 2:
            conv_out = result_sum.reshape(tile_rows, tile_cols, width).astype(jnp.bfloat16)
    part = (keep + came.astype(jnp.float32)).astype(jnp.bfloat16)
    for n in range(len(plan) - 1, 1, -1):
        other = step(part, plan[n][0], lats, lons)
        part = jnp.where(
            halves[n] == 0, jnp.concatenate([part, other]), jnp.concatenate([other, part])
        )
    own, beside = halves[1], kept_half(plan[1][1], lat ^ 1, lon)
    other = step(part, plan[1][0], lats, lons)
    beside_part = step(part, plan[0][0], lats, lons)
    beside_other = step(other, plan[0][0], lats, lons)
    totals = None
    for quarter, value in (
        (2 * core + own, part),
        (2 * (1 - core) + beside, beside_part),
        (2 * core + 1 - own, other),
        (2 * (1 - core) + 1 - beside, beside_other),
    ):
        totals = place(quarter, value, taps, width, channels, loss_scale, totals)
    conv_total, encoder_total, gain_total = totals
    gain_total = gain_total[0]
    return (conv_out, conv_total.reshape(3, 3, width, width), encoder_total, gain_total)


def solution(mesh):
    placed = (
        P(("lat", "lon"), None),
        P(("lat", "lon")),
        P(("lat", "lon")),
        P(("lat", "lon")),
        P(),
        P(),
        P(),
        P(),
        P("lat", "lon", None),
    )

    return jax.shard_map(
        shards,
        mesh=mesh,
        in_specs=placed,
        out_specs=(P("lat", "lon", None), P(), P(), P()),
        check_vma=False,
    )
```

```python
import math

import jax
import jax.numpy as jnp
from jax import lax
from jax.experimental import pallas as pl
from jax.experimental.pallas import tpu as pltpu
from jax.sharding import PartitionSpec as P


PH = 8
PW = 16
MOST = 3
EPS = 1e-06
LANES = 128
AXES = ("lat", "lon")
VMEM_LIMIT = 24 * 1024 * 1024


def bits_of(count):
    assert count & (count - 1) == 0
    return [1 << i for i in range(count.bit_length() - 1)]


def parity(value, mask):
    out = jnp.zeros((), jnp.int32)
    while mask:
        low = mask & -mask
        out = out ^ ((value & low) != 0).astype(jnp.int32)
        mask ^= low
    return out


def exchange(value, lats, lons, move):
    pairs = []
    for a in range(lats):
        for b in range(lons):
            c, d = move(a, b)
            pairs.append((a * lons + b, c * lons + d))
    return lax.ppermute(value, AXES, pairs)


def stage_plan(lats, lons):
    lat_bits, lon_bits = bits_of(lats), bits_of(lons)
    first = lat_bits[:1]
    lat_rest = lat_bits[1:]
    low, high = lon_bits[:1], lon_bits[1:]
    plan = [(((m, 0), (m, 0)), ((m, 0), (m, 0))) for m in first]
    ab = [(m, 0) for m in lat_rest] + [(0, m) for m in low]
    ba = [(0, m) for m in low] + [(m, 0) for m in lat_rest]
    plan += [((p, q), (p, q)) for p, q in zip(ab, ba)]
    if len(high) == 2:
        one, two = high
        plan += [(((0, one),) * 2, ((0, one | two),) * 2), (((0, one | two),) * 2, ((0, two),) * 2)]
    else:
        plan += [(((0, m),) * 2, ((0, m),) * 2) for m in high]
    return plan


def kept_half(masks, lat, lon):
    even = parity(lat, masks[0][0]) ^ parity(lon, masks[0][1])
    odd = parity(lat, masks[1][0]) ^ parity(lon, masks[1][1])
    return jnp.where((lat & 1) == 0, even, odd)


def step(value, steps, lats, lons):
    return exchange(value, lats, lons, lambda a, b: (a ^ steps[a & 1][0], b ^ steps[a & 1][1]))


def pick(value, half):
    pair = value.reshape(2, value.shape[0] // 2, value.shape[1])
    return lax.dynamic_index_in_dim(pair, half, 0, keepdims=False)


def split_sum(keep, came, half):
    away = pick(keep, 1 - half) + pick(came, 1 - half).astype(jnp.float32)
    stay = pick(keep, half) + pick(came, half).astype(jnp.float32)
    return away.astype(jnp.bfloat16), stay


def padded_2(shard, sides, width, wrap):
    for axis, dim in sides:
        size, length = (lax.axis_size(axis), shard.shape[dim])
        up = [(i, (i + 1) % size) for i in range(size if wrap else size - 1)]
        down = [(j, i) for i, j in up]
        last = lax.slice_in_dim(shard, length - width, length, axis=dim)
        leading = lax.slice_in_dim(shard, 0, width, axis=dim)
        before = lax.ppermute(last, axis, up)
        after = lax.ppermute(leading, axis, down)
        shard = jnp.concatenate([before, shard, after], axis=dim)
    return shard


def to_patches(tile):
    rows, cols, width = tile.shape
    shaped = tile.reshape(rows // PH, PH, cols // PW, PW, width)
    return shaped.transpose(0, 2, 1, 3, 4).reshape(-1, width)


def whole(shape):
    zeros = (0,) * len(shape)
    return pl.BlockSpec(shape, lambda *_: zeros, pipeline_mode=pl.Buffered(1))


def call(body, scalars, ins, outs, grid=(1,), in_specs=None, out_specs=None, scratch=(), alias=None):
    return pl.pallas_call(
        body,
        out_shape=outs,
        grid_spec=pltpu.PrefetchScalarGridSpec(
            num_scalar_prefetch=1,
            grid=grid,
            in_specs=in_specs or [whole(a.shape) for a in ins],
            out_specs=out_specs or [whole(o.shape) for o in outs],
            scratch_shapes=list(scratch),
        ),
        input_output_aliases=alias or {},
        compiler_params=pltpu.CompilerParams(vmem_limit_bytes=VMEM_LIMIT),
    )(scalars, *ins)


def shape_of(shape, dtype):
    return jax.ShapeDtypeStruct(shape, dtype)


def nt(left, right):
    return lax.dot_general(left, right, (((1,), (1,)), ((), ())), preferred_element_type=jnp.float32)


def lanes(at, size):
    return pl.ds(pl.multiple_of(at * size, size), size)


def pack(spectra_t, source, places, rows):
    channels = spectra_t.shape[0]

    def body(src, full, *refs):
        outs, sems = refs[:-1], refs[-1]
        copies = []
        for n, k in enumerate(places):
            for j in range(MOST):
                copies.append(
                    pltpu.make_async_copy(
                        full.at[:, lanes(src[k * MOST + j], rows)],
                        outs[n].at[:, j * rows : (j + 1) * rows],
                        sems.at[n * MOST + j],
                    )
                )
        for c in copies:
            c.start()
        for c in copies:
            c.wait()

    outs = [shape_of((channels, MOST * rows), spectra_t.dtype)] * len(places)
    return call(
        body,
        source,
        [spectra_t],
        outs,
        in_specs=[pl.BlockSpec(memory_space=pl.ANY)],
        scratch=[pltpu.SemaphoreType.DMA((len(places) * MOST,))],
    )


def spread_blocks(meta, first, arrived, weight_t, kernels, gain_col, before, patches, last):
    count = len(arrived)
    kernel_count, rows, cells = kernels.shape
    width = weight_t.shape[0]

    def body(meta_ref, *refs):
        xs = refs[:count]
        w, kern, g = refs[count : count + 3]
        spread, slope, *rest, enc = refs[count + 3 + (before is not None) :]
        if before is None:
            spread[...] = jnp.zeros_like(spread)
        else:
            spread[...] = refs[count + 3][...]
        for k in range(count):

            def encode(c, _, k=k):
                span = lanes(c, width // 2)
                pre = jnp.dot(w[span], xs[k][...], preferred_element_type=jnp.float32)
                s = jax.nn.sigmoid(pre)
                slope[k, span] = (s * (1.0 + pre * (1.0 - s))).astype(jnp.bfloat16)
                enc[span] = (pre * s).astype(jnp.bfloat16)
                return 0

            lax.fori_loop(0, 2, encode, 0)

            def add(j, _, k=k):
                code = meta_ref[(first + k) * MOST + j]

                @pl.when(code >= 0)
                def _():
                    spread[code // kernel_count] += jnp.dot(
                        enc[:, lanes(j, rows)],
                        kern[code % kernel_count],
                        preferred_element_type=jnp.float32,
                    )

                return 0

            lax.fori_loop(0, MOST, add, 0)

        if last:

            def norm(q, _):
                cell = spread[q]
                r = lax.rsqrt(jnp.mean(cell * cell, axis=0, keepdims=True) + EPS)
                rest[0][:, lanes(q, cells)] = (cell * r * g[...]).astype(jnp.bfloat16)
                return 0

            lax.fori_loop(0, patches, norm, 0)

    outs = [
        shape_of((patches, width, cells), jnp.float32),
        shape_of((count, width, MOST * rows), jnp.bfloat16),
    ]
    outs = [pltpu.HBM(o.shape, o.dtype) if last or n == 1 else o for n, o in enumerate(outs)]
    if last:
        outs.append(shape_of((width, patches * cells), jnp.bfloat16))
    ins = [*arrived, weight_t, kernels, gain_col] + ([] if before is None else [before])
    scratch = [pltpu.VMEM((width, MOST * rows), jnp.bfloat16)]
    return call(body, meta, ins, outs, scratch=scratch)


def backward(meta, arrived, kernels_t, gain_col, spread, slopes, d_normed_t):
    count = len(arrived)
    groups = len(slopes)
    place_of = [(n, k) for n, one in enumerate(slopes) for k in range(one.shape[0])]
    kernel_count, cells, rows = kernels_t.shape
    patches, width, _ = spread.shape
    channels = arrived[0].shape[0]

    def body(meta_ref, *refs):
        xs = refs[:count]
        slos = refs[count : count + groups]
        spr, dn, kern, g, out, dsp, dpre, xbuf, sbuf, spr_buf, dn_buf, sems, patch_sems = refs[
            count + groups :
        ]

        def field(q):
            return (
                pltpu.make_async_copy(spr.at[q], spr_buf.at[q], patch_sems.at[2 * q]),
                pltpu.make_async_copy(dn.at[:, lanes(q, cells)], dn_buf.at[q], patch_sems.at[2 * q + 1]),
            )

        for q in range(patches):
            for one in field(q):
                one.start()
        copies = []
        for k in range(count):
            n, at = place_of[k]
            copies.append(pltpu.make_async_copy(xs[k], xbuf.at[k], sems.at[2 * k]))
            copies.append(pltpu.make_async_copy(slos[n].at[at], sbuf.at[k], sems.at[2 * k + 1]))
        for one in copies:
            one.start()

        def unnorm(q, total):
            for one in field(q):
                one.wait()
            cell = spr_buf[q]
            d = dn_buf[q]
            r = lax.rsqrt(jnp.mean(cell * cell, axis=0, keepdims=True) + EPS)
            unit = cell * r
            dg = d * g[...]
            inner = jnp.mean(dg * unit, axis=0, keepdims=True)
            dsp[q] = ((dg - unit * inner) * r).astype(jnp.bfloat16)
            return total + jnp.sum(d * unit, axis=1, keepdims=True)

        total = lax.fori_loop(0, patches, unnorm, jnp.zeros((width, 1), jnp.float32))
        out[...] = jnp.zeros_like(out)
        out[:, channels : channels + 1] = total

        def arrival(k, _):
            pltpu.make_async_copy(xbuf.at[k], xbuf.at[k], sems.at[2 * k]).wait()
            pltpu.make_async_copy(sbuf.at[k], sbuf.at[k], sems.at[2 * k + 1]).wait()

            def back(j, _):
                code = meta_ref[k * MOST + j]
                span = lanes(j, rows)

                @pl.when(code >= 0)
                def _():
                    drow = jnp.dot(
                        dsp[code // kernel_count],
                        kern[code % kernel_count],
                        preferred_element_type=jnp.float32,
                    ).astype(jnp.bfloat16)
                    dpre[:, span] = (
                        drow.astype(jnp.float32) * sbuf[k, :, span].astype(jnp.float32)
                    ).astype(jnp.bfloat16)

                @pl.when(code < 0)
                def _():
                    dpre[:, span] = jnp.zeros((width, rows), jnp.bfloat16)

                return 0

            lax.fori_loop(0, MOST, back, 0)
            out[:, :channels] += nt(dpre[...], xbuf[k])
            return 0

        lax.fori_loop(0, count, arrival, 0)

    held = [pltpu.with_memory_space_constraint(x, pltpu.HBM) for x in (*slopes, spread, d_normed_t)]
    ins = [*arrived, *held, kernels_t, gain_col]
    outs = [shape_of((width, (channels // LANES + 1) * LANES), jnp.float32)]
    scratch = [
        pltpu.VMEM((patches, width, cells), jnp.bfloat16),
        pltpu.VMEM((width, MOST * rows), jnp.bfloat16),
        pltpu.VMEM((count, channels, MOST * rows), jnp.bfloat16),
        pltpu.VMEM((count, width, MOST * rows), jnp.bfloat16),
        pltpu.VMEM((patches, width, cells), jnp.float32),
        pltpu.VMEM((patches, width, cells), jnp.float32),
        pltpu.SemaphoreType.DMA((2 * count,)),
        pltpu.SemaphoreType.DMA((2 * patches,)),
    ]
    far = [pl.BlockSpec(memory_space=pltpu.HBM)] * (count + groups + 2)
    in_specs = far + [whole(a.shape) for a in ins[count + groups + 2 :]]
    return call(body, meta, ins, outs, in_specs=in_specs, scratch=scratch)[0]


def place(quarter, part, taps, lane, channels, scale, into=None):
    rows = part.shape[0]
    steps = 2
    unit = rows // steps

    def body(at, piece, small, *refs):
        conv, encoder, gain = refs[-3:]
        for t in range(taps):
            conv[t] = piece[:, t * lane : (t + 1) * lane].astype(jnp.float32) * scale

        @pl.when(pl.program_id(0) == 0)
        def _():
            turned = (small[:, taps * lane :].astype(jnp.float32) * scale).T
            encoder[...] = turned[:channels]
            gain[...] = turned[channels : channels + 1]

    specs = [pl.BlockSpec((unit, part.shape[1]), lambda i, q: (i, 0)), whole(part.shape)]
    ins = [part, part]
    if into is not None:
        ins += list(into)
        specs += [pl.BlockSpec(memory_space=pl.ANY)] * 3
    return call(
        body,
        quarter.reshape(1),
        ins,
        [
            shape_of((taps, 4 * rows, lane), jnp.float32),
            shape_of((channels, 4 * rows), jnp.float32),
            shape_of((1, 4 * rows), jnp.float32),
        ],
        grid=(steps,),
        in_specs=specs,
        out_specs=[
            pl.BlockSpec((taps, unit, lane), lambda i, q: (0, q[0] * steps + i, 0)),
            pl.BlockSpec((channels, rows), lambda i, q: (0, q[0])),
            pl.BlockSpec((1, rows), lambda i, q: (0, q[0])),
        ],
        alias=None if into is None else {3: 0, 4: 1, 5: 2},
    )


def shards(
    spectra,
    block_target,
    block_patch,
    block_kernel,
    encoder_weight,
    kernels,
    gain,
    conv_weight,
    cotangent,
):
    lons = lax.axis_size("lon")
    lats = lax.axis_size("lat")
    lon = lax.axis_index("lon")
    blocks = block_target.shape[0]
    kernel_count, block_rows, _ = kernels.shape
    channels = spectra.shape[1]
    width = encoder_weight.shape[1]
    tile_rows, tile_cols = (cotangent.shape[0], cotangent.shape[1])
    loss_scale = 1.0 / math.sqrt(tile_rows * lats * tile_cols * lons)
    cells = tile_rows * tile_cols

    cot_beside = padded_2(cotangent, (("lon", 1),), 1, True)
    order = lon ^ jnp.arange(lons, dtype=jnp.int32)
    hit = (block_target[:, None] == order[None, :]).astype(jnp.int32)
    rank = jnp.cumsum(hit, axis=0) - hit
    chosen = hit[:, :, None] * (rank[:, :, None] == jnp.arange(MOST)[None, None, :]).astype(jnp.int32)
    number = jnp.arange(blocks, dtype=jnp.int32)
    source = jnp.sum(chosen * number[:, None, None], axis=0).reshape(-1)
    code = block_patch * kernel_count + block_kernel + 1
    codes = jnp.sum(chosen * code[:, None, None], axis=0) - 1
    spectra_t = spectra.T
    far, near = range(lons // 2, lons), range(lons // 2)
    packed = dict(zip(far, pack(spectra_t, source, far, block_rows)))
    packed |= zip(near, pack(spectra_t, source, near, block_rows))
    cot_padded = padded_2(cot_beside, (("lat", 0),), 1, False)

    by_tile = jnp.sum(
        jnp.where((order[None, :] == jnp.arange(lons)[:, None])[:, :, None], codes[None], 0), axis=1
    )
    came = lax.all_to_all(by_tile, "lon", 0, 0, tiled=True)
    meta = jnp.sum(
        jnp.where((order[:, None] == jnp.arange(lons)[None, :])[:, :, None], came[None], 0), axis=1
    ).reshape(-1)

    arrived = [packed[0]] + [None] * (lons - 1)
    for k in [*far, *near[1:]]:
        arrived[k] = exchange(packed[k], lats, lons, lambda a, b, k=k: (a, b ^ k))

    windows = jnp.concatenate(
        [
            to_patches(cot_padded[2 - a : 2 - a + tile_rows, 2 - b : 2 - b + tile_cols])
            for a in range(3)
            for b in range(3)
        ],
        axis=1,
    )
    taps = 9
    weight_all = conv_weight.reshape(taps, width, width).transpose(1, 0, 2).reshape(width, -1)
    d_normed_t = nt(weight_all, windows)

    meta, d_normed_t, windows = lax.optimization_barrier((meta, d_normed_t, windows))
    arrived = [pltpu.with_memory_space_constraint(x, pltpu.HBM) for x in arrived]
    d_normed_t = pltpu.with_memory_space_constraint(d_normed_t, pltpu.HBM)
    patches = tile_rows // PH * (tile_cols // PW)
    gain_col = gain.reshape(width, 1)
    weight_t = encoder_weight.T
    cuts = [0, lons // 2, lons - 1, lons]
    spread, slopes = None, []
    for low, high in zip(cuts, cuts[1:]):
        last = high == lons
        spread, slope, *rest = spread_blocks(
            meta, low, arrived[low:high], weight_t, kernels, gain_col, spread, patches, last
        )
        slopes.append(slope)
    normed_t = rest[0]

    plan = stage_plan(lats, lons)
    lat = lax.axis_index("lat")
    halves = [kept_half(masks, lat, lon) for _, masks in plan]
    core = halves[0]
    away = jnp.dot(
        pick(normed_t, 1 - core), windows, preferred_element_type=jnp.float32
    ).astype(jnp.bfloat16)
    keep = jnp.dot(pick(normed_t, core), windows, preferred_element_type=jnp.float32)
    came = step(away, plan[0][0], lats, lons)

    away, keep = split_sum(keep, came, halves[1])
    away, spread, normed_after = lax.optimization_barrier((away, spread, normed_t))
    came = step(away, plan[1][0], lats, lons)
    kernels_t = kernels.transpose(0, 2, 1)
    small = backward(meta, arrived, kernels_t, gain_col, spread, slopes, d_normed_t)
    small_keep = pick(small, core)
    small_came = step(pick(small, 1 - core).astype(jnp.bfloat16), plan[0][0], lats, lons)

    away, small_keep = split_sum(small_keep, small_came, halves[1])
    small_came = step(away, plan[1][0], lats, lons)
    apart = len(plan) - 2
    for n in range(2, apart):
        away, keep = split_sum(keep, came, halves[n])
        came = step(away, plan[n][0], lats, lons)
        away, small_keep = split_sum(small_keep, small_came, halves[n])
        small_came = step(away, plan[n][0], lats, lons)
    keep = jnp.concatenate([keep, small_keep], axis=1)
    came = jnp.concatenate([came, small_came], axis=1)
    for n in range(apart, len(plan)):
        away, keep = split_sum(keep, came, halves[n])
        came = step(away, plan[n][0], lats, lons)
    normed = normed_after.reshape(width, tile_rows // PH, tile_cols // PW, PH, PW)
    normed = normed.transpose(1, 3, 2, 4, 0).reshape(tile_rows, tile_cols, width)
    padded = padded_2(normed, (("lon", 1),), 1, True)
    padded = padded_2(padded, (("lat", 0),), 1, False)
    result_sum = jnp.zeros((cells, width), jnp.float32)
    for a in range(3):
        for b in range(3):
            window = padded[a : a + tile_rows, b : b + tile_cols].reshape(-1, width)
            result_sum = result_sum + jnp.dot(
                window, conv_weight[a, b], preferred_element_type=jnp.float32
            )
        if a == 2:
            conv_out = result_sum.reshape(tile_rows, tile_cols, width).astype(jnp.bfloat16)
    part = (keep + came.astype(jnp.float32)).astype(jnp.bfloat16)
    for n in range(len(plan) - 1, 1, -1):
        other = step(part, plan[n][0], lats, lons)
        part = jnp.where(
            halves[n] == 0, jnp.concatenate([part, other]), jnp.concatenate([other, part])
        )
    own, beside = halves[1], kept_half(plan[1][1], lat ^ 1, lon)
    other = step(part, plan[1][0], lats, lons)
    beside_part = step(part, plan[0][0], lats, lons)
    beside_other = step(other, plan[0][0], lats, lons)
    totals = None
    for quarter, value in (
        (2 * core + own, part),
        (2 * (1 - core) + beside, beside_part),
        (2 * core + 1 - own, other),
        (2 * (1 - core) + 1 - beside, beside_other),
    ):
        totals = place(quarter, value, taps, width, channels, loss_scale, totals)
    conv_total, encoder_total, gain_total = totals
    gain_total = gain_total[0]
    return (conv_out, conv_total.reshape(3, 3, width, width), encoder_total, gain_total)


def solution(mesh):
    placed = (
        P(("lat", "lon"), None),
        P(("lat", "lon")),
        P(("lat", "lon")),
        P(("lat", "lon")),
        P(),
        P(),
        P(),
        P(),
        P("lat", "lon", None),
    )

    return jax.shard_map(
        shards,
        mesh=mesh,
        in_specs=placed,
        out_specs=(P("lat", "lon", None), P(), P(), P()),
        check_vma=False,
    )
```

```python
import math

import jax
import jax.numpy as jnp
from jax import lax
from jax.experimental import pallas as pl
from jax.experimental.pallas import tpu as pltpu
from jax.sharding import PartitionSpec as P


PH = 8
PW = 16
MOST = 3
EPS = 1e-06
LANES = 128
AXES = ("lat", "lon")
VMEM_LIMIT = 24 * 1024 * 1024


def bits_of(count):
    assert count & (count - 1) == 0
    return [1 << i for i in range(count.bit_length() - 1)]


def parity(value, mask):
    out = jnp.zeros((), jnp.int32)
    while mask:
        low = mask & -mask
        out = out ^ ((value & low) != 0).astype(jnp.int32)
        mask ^= low
    return out


def exchange(value, lats, lons, move):
    pairs = []
    for a in range(lats):
        for b in range(lons):
            c, d = move(a, b)
            pairs.append((a * lons + b, c * lons + d))
    return lax.ppermute(value, AXES, pairs)


def stage_plan(lats, lons):
    lat_bits, lon_bits = bits_of(lats), bits_of(lons)
    first = lat_bits[:1]
    lat_rest = lat_bits[1:]
    low, high = lon_bits[:1], lon_bits[1:]
    plan = [(((m, 0), (m, 0)), ((m, 0), (m, 0))) for m in first]
    ab = [(m, 0) for m in lat_rest] + [(0, m) for m in low]
    ba = [(0, m) for m in low] + [(m, 0) for m in lat_rest]
    plan += [((p, q), (p, q)) for p, q in zip(ab, ba)]
    if len(high) == 2:
        one, two = high
        plan += [(((0, one),) * 2, ((0, one | two),) * 2), (((0, one | two),) * 2, ((0, two),) * 2)]
    else:
        plan += [(((0, m),) * 2, ((0, m),) * 2) for m in high]
    return plan


def kept_half(masks, lat, lon):
    even = parity(lat, masks[0][0]) ^ parity(lon, masks[0][1])
    odd = parity(lat, masks[1][0]) ^ parity(lon, masks[1][1])
    return jnp.where((lat & 1) == 0, even, odd)


def step(value, steps, lats, lons):
    return exchange(value, lats, lons, lambda a, b: (a ^ steps[a & 1][0], b ^ steps[a & 1][1]))


def pick(value, half):
    pair = value.reshape(2, value.shape[0] // 2, value.shape[1])
    return lax.dynamic_index_in_dim(pair, half, 0, keepdims=False)


def split_sum(keep, came, half):
    away = pick(keep, 1 - half) + pick(came, 1 - half).astype(jnp.float32)
    stay = pick(keep, half) + pick(came, half).astype(jnp.float32)
    return away.astype(jnp.bfloat16), stay


def padded_2(shard, sides, width, wrap):
    for axis, dim in sides:
        size, length = (lax.axis_size(axis), shard.shape[dim])
        up = [(i, (i + 1) % size) for i in range(size if wrap else size - 1)]
        down = [(j, i) for i, j in up]
        last = lax.slice_in_dim(shard, length - width, length, axis=dim)
        leading = lax.slice_in_dim(shard, 0, width, axis=dim)
        before = lax.ppermute(last, axis, up)
        after = lax.ppermute(leading, axis, down)
        shard = jnp.concatenate([before, shard, after], axis=dim)
    return shard


def to_patches(tile):
    rows, cols, width = tile.shape
    shaped = tile.reshape(rows // PH, PH, cols // PW, PW, width)
    return shaped.transpose(0, 2, 1, 3, 4).reshape(-1, width)


def whole(shape):
    zeros = (0,) * len(shape)
    return pl.BlockSpec(shape, lambda *_: zeros, pipeline_mode=pl.Buffered(1))


def call(body, scalars, ins, outs, grid=(1,), in_specs=None, out_specs=None, scratch=(), alias=None):
    return pl.pallas_call(
        body,
        out_shape=outs,
        grid_spec=pltpu.PrefetchScalarGridSpec(
            num_scalar_prefetch=1,
            grid=grid,
            in_specs=in_specs or [whole(a.shape) for a in ins],
            out_specs=out_specs or [whole(o.shape) for o in outs],
            scratch_shapes=list(scratch),
        ),
        input_output_aliases=alias or {},
        compiler_params=pltpu.CompilerParams(vmem_limit_bytes=VMEM_LIMIT),
    )(scalars, *ins)


def shape_of(shape, dtype):
    return jax.ShapeDtypeStruct(shape, dtype)


def nt(left, right):
    return lax.dot_general(left, right, (((1,), (1,)), ((), ())), preferred_element_type=jnp.float32)


def lanes(at, size):
    return pl.ds(pl.multiple_of(at * size, size), size)


def pack(spectra_t, source, places, rows):
    channels = spectra_t.shape[0]

    def body(src, full, *refs):
        outs, sems = refs[:-1], refs[-1]
        copies = []
        for n, k in enumerate(places):
            for j in range(MOST):
                copies.append(
                    pltpu.make_async_copy(
                        full.at[:, lanes(src[k * MOST + j], rows)],
                        outs[n].at[:, j * rows : (j + 1) * rows],
                        sems.at[n * MOST + j],
                    )
                )
        for c in copies:
            c.start()
        for c in copies:
            c.wait()

    outs = [shape_of((channels, MOST * rows), spectra_t.dtype)] * len(places)
    return call(
        body,
        source,
        [spectra_t],
        outs,
        in_specs=[pl.BlockSpec(memory_space=pl.ANY)],
        scratch=[pltpu.SemaphoreType.DMA((len(places) * MOST,))],
    )


def spread_blocks(meta, first, arrived, weight_t, kernels, gain_col, before, patches, last):
    count = len(arrived)
    kernel_count, rows, cells = kernels.shape
    width = weight_t.shape[0]

    def body(meta_ref, *refs):
        xs = refs[:count]
        w, kern, g = refs[count : count + 3]
        spread, slope, *rest, enc = refs[count + 3 + (before is not None) :]
        if before is None:
            spread[...] = jnp.zeros_like(spread)
        else:
            spread[...] = refs[count + 3][...]
        for k in range(count):
            pre = jnp.dot(w[...], xs[k][...], preferred_element_type=jnp.float32)
            s = jax.nn.sigmoid(pre)
            slope[k] = (s * (1.0 + pre * (1.0 - s))).astype(jnp.bfloat16)
            enc[...] = (pre * s).astype(jnp.bfloat16)

            def add(j, _, k=k):
                code = meta_ref[(first + k) * MOST + j]

                @pl.when(code >= 0)
                def _():
                    spread[code // kernel_count] += jnp.dot(
                        enc[:, lanes(j, rows)],
                        kern[code % kernel_count],
                        preferred_element_type=jnp.float32,
                    )

                return 0

            lax.fori_loop(0, MOST, add, 0)

        if last:

            def norm(q, _):
                cell = spread[q]
                r = lax.rsqrt(jnp.mean(cell * cell, axis=0, keepdims=True) + EPS)
                rest[0][:, lanes(q, cells)] = (cell * r * g[...]).astype(jnp.bfloat16)
                return 0

            lax.fori_loop(0, patches, norm, 0)

    outs = [
        shape_of((patches, width, cells), jnp.float32),
        shape_of((count, width, MOST * rows), jnp.bfloat16),
    ]
    outs = [pltpu.HBM(o.shape, o.dtype) if last or n == 1 else o for n, o in enumerate(outs)]
    if last:
        outs.append(shape_of((width, patches * cells), jnp.bfloat16))
    ins = [*arrived, weight_t, kernels, gain_col] + ([] if before is None else [before])
    scratch = [pltpu.VMEM((width, MOST * rows), jnp.bfloat16)]
    return call(body, meta, ins, outs, scratch=scratch)


def backward(meta, arrived, kernels_t, gain_col, spread, slopes, d_normed_t):
    count = len(arrived)
    groups = len(slopes)
    place_of = [(n, k) for n, one in enumerate(slopes) for k in range(one.shape[0])]
    kernel_count, cells, rows = kernels_t.shape
    patches, width, _ = spread.shape
    channels = arrived[0].shape[0]

    def body(meta_ref, *refs):
        xs = refs[:count]
        slos = refs[count : count + groups]
        spr, dn, kern, g, out, dsp, dpre, xbuf, sbuf, spr_buf, dn_buf, sems, patch_sems = refs[
            count + groups :
        ]

        def field(q):
            return (
                pltpu.make_async_copy(spr.at[q], spr_buf.at[q], patch_sems.at[2 * q]),
                pltpu.make_async_copy(dn.at[:, lanes(q, cells)], dn_buf.at[q], patch_sems.at[2 * q + 1]),
            )

        for q in range(patches):
            for one in field(q):
                one.start()
        copies = []
        for k in range(count):
            n, at = place_of[k]
            copies.append(pltpu.make_async_copy(xs[k], xbuf.at[k], sems.at[2 * k]))
            copies.append(pltpu.make_async_copy(slos[n].at[at], sbuf.at[k], sems.at[2 * k + 1]))
        for one in copies:
            one.start()

        def unnorm(q, total):
            for one in field(q):
                one.wait()
            cell = spr_buf[q]
            d = dn_buf[q]
            r = lax.rsqrt(jnp.mean(cell * cell, axis=0, keepdims=True) + EPS)
            unit = cell * r
            dg = d * g[...]
            inner = jnp.mean(dg * unit, axis=0, keepdims=True)
            dsp[q] = ((dg - unit * inner) * r).astype(jnp.bfloat16)
            return total + jnp.sum(d * unit, axis=1, keepdims=True)

        total = lax.fori_loop(0, patches, unnorm, jnp.zeros((width, 1), jnp.float32))
        out[...] = jnp.zeros_like(out)
        out[:, channels : channels + 1] = total
        for k in range(count):
            copies[2 * k].wait()
            copies[2 * k + 1].wait()

            def back(j, _, k=k):
                code = meta_ref[k * MOST + j]
                span = lanes(j, rows)

                @pl.when(code >= 0)
                def _():
                    drow = jnp.dot(
                        dsp[code // kernel_count],
                        kern[code % kernel_count],
                        preferred_element_type=jnp.float32,
                    ).astype(jnp.bfloat16)
                    dpre[:, span] = (
                        drow.astype(jnp.float32) * sbuf[k, :, span].astype(jnp.float32)
                    ).astype(jnp.bfloat16)

                @pl.when(code < 0)
                def _():
                    dpre[:, span] = jnp.zeros((width, rows), jnp.bfloat16)

                return 0

            lax.fori_loop(0, MOST, back, 0)
            out[:, :channels] += nt(dpre[...], xbuf[k])

    held = [pltpu.with_memory_space_constraint(x, pltpu.HBM) for x in (*slopes, spread, d_normed_t)]
    ins = [*arrived, *held, kernels_t, gain_col]
    outs = [shape_of((width, (channels // LANES + 1) * LANES), jnp.float32)]
    scratch = [
        pltpu.VMEM((patches, width, cells), jnp.bfloat16),
        pltpu.VMEM((width, MOST * rows), jnp.bfloat16),
        pltpu.VMEM((count, channels, MOST * rows), jnp.bfloat16),
        pltpu.VMEM((count, width, MOST * rows), jnp.bfloat16),
        pltpu.VMEM((patches, width, cells), jnp.float32),
        pltpu.VMEM((patches, width, cells), jnp.float32),
        pltpu.SemaphoreType.DMA((2 * count,)),
        pltpu.SemaphoreType.DMA((2 * patches,)),
    ]
    far = [pl.BlockSpec(memory_space=pltpu.HBM)] * (count + groups + 2)
    in_specs = far + [whole(a.shape) for a in ins[count + groups + 2 :]]
    return call(body, meta, ins, outs, in_specs=in_specs, scratch=scratch)[0]


def place(quarter, part, taps, lane, channels, scale, into=None):
    rows = part.shape[0]
    steps = 2
    unit = rows // steps

    def body(at, piece, small, *refs):
        conv, encoder, gain = refs[-3:]
        for t in range(taps):
            conv[t] = piece[:, t * lane : (t + 1) * lane].astype(jnp.float32) * scale

        @pl.when(pl.program_id(0) == 0)
        def _():
            turned = (small[:, taps * lane :].astype(jnp.float32) * scale).T
            encoder[...] = turned[:channels]
            gain[...] = turned[channels : channels + 1]

    specs = [pl.BlockSpec((unit, part.shape[1]), lambda i, q: (i, 0)), whole(part.shape)]
    ins = [part, part]
    if into is not None:
        ins += list(into)
        specs += [pl.BlockSpec(memory_space=pl.ANY)] * 3
    return call(
        body,
        quarter.reshape(1),
        ins,
        [
            shape_of((taps, 4 * rows, lane), jnp.float32),
            shape_of((channels, 4 * rows), jnp.float32),
            shape_of((1, 4 * rows), jnp.float32),
        ],
        grid=(steps,),
        in_specs=specs,
        out_specs=[
            pl.BlockSpec((taps, unit, lane), lambda i, q: (0, q[0] * steps + i, 0)),
            pl.BlockSpec((channels, rows), lambda i, q: (0, q[0])),
            pl.BlockSpec((1, rows), lambda i, q: (0, q[0])),
        ],
        alias=None if into is None else {3: 0, 4: 1, 5: 2},
    )


def shards(
    spectra,
    block_target,
    block_patch,
    block_kernel,
    encoder_weight,
    kernels,
    gain,
    conv_weight,
    cotangent,
):
    lons = lax.axis_size("lon")
    lats = lax.axis_size("lat")
    lon = lax.axis_index("lon")
    blocks = block_target.shape[0]
    kernel_count, block_rows, _ = kernels.shape
    channels = spectra.shape[1]
    width = encoder_weight.shape[1]
    tile_rows, tile_cols = (cotangent.shape[0], cotangent.shape[1])
    loss_scale = 1.0 / math.sqrt(tile_rows * lats * tile_cols * lons)
    cells = tile_rows * tile_cols

    cot_beside = padded_2(cotangent, (("lon", 1),), 1, True)
    order = lon ^ jnp.arange(lons, dtype=jnp.int32)
    hit = (block_target[:, None] == order[None, :]).astype(jnp.int32)
    rank = jnp.cumsum(hit, axis=0) - hit
    chosen = hit[:, :, None] * (rank[:, :, None] == jnp.arange(MOST)[None, None, :]).astype(jnp.int32)
    number = jnp.arange(blocks, dtype=jnp.int32)
    source = jnp.sum(chosen * number[:, None, None], axis=0).reshape(-1)
    code = block_patch * kernel_count + block_kernel + 1
    codes = jnp.sum(chosen * code[:, None, None], axis=0) - 1
    spectra_t = pltpu.with_memory_space_constraint(spectra.T, pltpu.HBM)
    far, near = range(lons // 2, lons), range(lons // 2)
    packed = dict(zip(far, pack(spectra_t, source, far, block_rows)))
    packed |= zip(near, pack(spectra_t, source, near, block_rows))
    cot_padded = padded_2(cot_beside, (("lat", 0),), 1, False)

    by_tile = jnp.sum(
        jnp.where((order[None, :] == jnp.arange(lons)[:, None])[:, :, None], codes[None], 0), axis=1
    )
    came = lax.all_to_all(by_tile, "lon", 0, 0, tiled=True)
    meta = jnp.sum(
        jnp.where((order[:, None] == jnp.arange(lons)[None, :])[:, :, None], came[None], 0), axis=1
    ).reshape(-1)

    arrived = [packed[0]] + [None] * (lons - 1)
    for k in [*far, *near[1:]]:
        arrived[k] = exchange(packed[k], lats, lons, lambda a, b, k=k: (a, b ^ k))

    windows = jnp.concatenate(
        [
            to_patches(cot_padded[2 - a : 2 - a + tile_rows, 2 - b : 2 - b + tile_cols])
            for a in range(3)
            for b in range(3)
        ],
        axis=1,
    )
    taps = 9
    weight_all = conv_weight.reshape(taps, width, width).transpose(1, 0, 2).reshape(width, -1)
    d_normed_t = nt(weight_all, windows)

    meta, d_normed_t, windows = lax.optimization_barrier((meta, d_normed_t, windows))
    arrived = [pltpu.with_memory_space_constraint(x, pltpu.HBM) for x in arrived]
    d_normed_t = pltpu.with_memory_space_constraint(d_normed_t, pltpu.HBM)
    patches = tile_rows // PH * (tile_cols // PW)
    gain_col = gain.reshape(width, 1)
    weight_t = encoder_weight.T
    cuts = [0, lons // 2, lons - 1, lons]
    spread, slopes = None, []
    for low, high in zip(cuts, cuts[1:]):
        last = high == lons
        spread, slope, *rest = spread_blocks(
            meta, low, arrived[low:high], weight_t, kernels, gain_col, spread, patches, last
        )
        slopes.append(slope)
    normed_t = rest[0]

    plan = stage_plan(lats, lons)
    lat = lax.axis_index("lat")
    halves = [kept_half(masks, lat, lon) for _, masks in plan]
    core = halves[0]
    away = jnp.dot(
        pick(normed_t, 1 - core), windows, preferred_element_type=jnp.float32
    ).astype(jnp.bfloat16)
    keep = jnp.dot(pick(normed_t, core), windows, preferred_element_type=jnp.float32)
    came = step(away, plan[0][0], lats, lons)

    away, keep = split_sum(keep, came, halves[1])
    away, spread, normed_after = lax.optimization_barrier((away, spread, normed_t))
    came = step(away, plan[1][0], lats, lons)
    kernels_t = kernels.transpose(0, 2, 1)
    small = backward(meta, arrived, kernels_t, gain_col, spread, slopes, d_normed_t)
    small_keep = pick(small, core)
    small_came = step(pick(small, 1 - core).astype(jnp.bfloat16), plan[0][0], lats, lons)

    away, small_keep = split_sum(small_keep, small_came, halves[1])
    small_came = step(away, plan[1][0], lats, lons)
    apart = len(plan) - 2
    for n in range(2, apart):
        away, keep = split_sum(keep, came, halves[n])
        came = step(away, plan[n][0], lats, lons)
        away, small_keep = split_sum(small_keep, small_came, halves[n])
        small_came = step(away, plan[n][0], lats, lons)
    keep = jnp.concatenate([keep, small_keep], axis=1)
    came = jnp.concatenate([came, small_came], axis=1)
    for n in range(apart, len(plan)):
        away, keep = split_sum(keep, came, halves[n])
        came = step(away, plan[n][0], lats, lons)
    normed = normed_after.reshape(width, tile_rows // PH, tile_cols // PW, PH, PW)
    normed = normed.transpose(1, 3, 2, 4, 0).reshape(tile_rows, tile_cols, width)
    padded = padded_2(normed, (("lon", 1),), 1, True)
    padded = padded_2(padded, (("lat", 0),), 1, False)
    result_sum = jnp.zeros((cells, width), jnp.float32)
    for a in range(3):
        for b in range(3):
            window = padded[a : a + tile_rows, b : b + tile_cols].reshape(-1, width)
            result_sum = result_sum + jnp.dot(
                window, conv_weight[a, b], preferred_element_type=jnp.float32
            )
        if a == 2:
            conv_out = result_sum.reshape(tile_rows, tile_cols, width).astype(jnp.bfloat16)
    part = (keep + came.astype(jnp.float32)).astype(jnp.bfloat16)
    for n in range(len(plan) - 1, 1, -1):
        other = step(part, plan[n][0], lats, lons)
        part = jnp.where(
            halves[n] == 0, jnp.concatenate([part, other]), jnp.concatenate([other, part])
        )
    own, beside = halves[1], kept_half(plan[1][1], lat ^ 1, lon)
    other = step(part, plan[1][0], lats, lons)
    beside_part = step(part, plan[0][0], lats, lons)
    beside_other = step(other, plan[0][0], lats, lons)
    totals = None
    for quarter, value in (
        (2 * core + own, part),
        (2 * (1 - core) + beside, beside_part),
        (2 * core + 1 - own, other),
        (2 * (1 - core) + 1 - beside, beside_other),
    ):
        totals = place(quarter, value, taps, width, channels, loss_scale, totals)
    conv_total, encoder_total, gain_total = totals
    gain_total = gain_total[0]
    return (conv_out, conv_total.reshape(3, 3, width, width), encoder_total, gain_total)


def solution(mesh):
    placed = (
        P(("lat", "lon"), None),
        P(("lat", "lon")),
        P(("lat", "lon")),
        P(("lat", "lon")),
        P(),
        P(),
        P(),
        P(),
        P("lat", "lon", None),
    )

    return jax.shard_map(
        shards,
        mesh=mesh,
        in_specs=placed,
        out_specs=(P("lat", "lon", None), P(), P(), P()),
        check_vma=False,
    )
```
